512 devices in a mesh: aux: 64 (over z, y), occ: 8 (over x, core).
Axes of the slice: x: 4, y: 8, z: 8, core: 2. Of those that a mesh axis runs over, the one named last changes fastest.
Arguments:
- integrals: bfloat16 [128, 21, 512, 512], P('aux', None, 'occ'), may hold values from -0.40234375 to 0.40234375
- orbitals: bfloat16 [3072, 384], replicated, may hold values from -0.109375 to 0.109375
Outputs:
- k_tiles: float32 [512, 21, 512], P('aux', None, 'occ')
The draws below stay inside these ranges and needn't reach their ends.
All inputs are finite; a program needn't handle non-finite values.
Results may differ from the reference program's by a relative error of at most 0.0017.
Values may be sent and summed in bfloat16 or wider, within the bound.
No kernel may reach another device: no remote copies, remote signals or barrier semaphores. Data moves between devices by JAX's collectives and lax.ppermute only.
A program may use at most 64 MiB of HBM per device.

```python
import jax
import jax.numpy as jnp
from jax import lax

TILE = 512
NB = 6
OCC = 384
NAUX = 128
N = 3072
NT = 21


def block_scale(own_key, dims, shards, smallest, top_value):
    def one(axis_at, parts):
        steps = jax.random.uniform(jax.random.fold_in(jax.random.fold_in(own_key, 6), axis_at), (parts,), jnp.float32, smallest / len(shards), top_value / len(shards))
        return jnp.repeat(jnp.exp(steps), dims[axis_at] // parts).reshape((-1,) + (1,) * (len(dims) - axis_at - 1))

    level = one(*shards[0])
    for cut in shards[1:]:
        level = level * one(*cut)
    return level


def bell_draw(own_key, extent, width, reach, cuts=(), held_as=jnp.bfloat16):
    array = width * jax.random.normal(own_key, extent, jnp.float32)
    if cuts:
        array = array * block_scale(own_key, extent, cuts, -0.22, 0.18)
    return jnp.clip(array, -reach, reach).astype(held_as)


def setup_inputs(seed: int = 0) -> dict:
    key_list = jax.random.split(jax.random.key(seed), 3)
    return {
        "integrals": bell_draw(key_list[0], (NAUX, NT, TILE, TILE), ((NAUX * OCC) ** -0.25), 0.40234375, ((0, 64), (2, 8))),
        "orbitals": bell_draw(key_list[1], (N, OCC), N ** -0.5, 0.109375),
    }


def tile_index(row_index, col_index):
    return row_index * NB - row_index * (row_index - 1) // 2 + col_index - row_index


def reference(integrals, orbitals):
    coeffs = orbitals.astype(jnp.float32)

    def per_slab(slab_tiles):
        band_list = []
        for row_index in range(NB):
            pieces = []
            for col_index in range(NB):
                if col_index >= row_index:
                    pieces.append(slab_tiles[tile_index(row_index, col_index)])
                else:
                    pieces.append(slab_tiles[tile_index(col_index, row_index)].T)
            band_list.append(jnp.concatenate(pieces, axis=1))
        full_matrix = jnp.concatenate(band_list, axis=0).astype(jnp.float32)
        return jnp.dot(full_matrix, coeffs, precision=lax.Precision.HIGHEST).astype(jnp.bfloat16)

    half_transform = lax.map(per_slab, integrals)
    flat_half = jnp.transpose(half_transform, (1, 0, 2)).reshape(NB * TILE, -1).astype(jnp.float32)
    exchange = jnp.dot(flat_half, flat_half.T, precision=lax.Precision.HIGHEST)
    out_tiles = []
    for row_index in range(NB):
        for col_index in range(row_index, NB):
            out_tiles.append(exchange[row_index * TILE:(row_index + 1) * TILE, col_index * TILE:(col_index + 1) * TILE])
    return jnp.stack(out_tiles, axis=1)
```

```python
import jax
import jax.numpy as jnp
from jax import lax
from jax.experimental import pallas as pl
from jax.experimental.pallas import tpu as pltpu
from jax.sharding import Mesh
from jax.sharding import PartitionSpec as P

NB = 6
F32 = jnp.float32
BF16 = jnp.bfloat16
VMEM = pl.BlockSpec(memory_space=pltpu.VMEM)


def tile_of(a, b):
    return a * NB - a * (a - 1) // 2 + b - a


OFF = [(a, b) for a in range(NB) for b in range(a + 1, NB)]
OFF_AT = {pair: at for at, pair in enumerate(OFF)}


def call(kernel, out_shape, args, flops, nbytes, vmem_mib):
    return pl.pallas_call(
        kernel,
        out_shape=out_shape,
        in_specs=[VMEM] * len(args),
        out_specs=jax.tree.map(lambda _: VMEM, out_shape),
        compiler_params=pltpu.CompilerParams(vmem_limit_bytes=vmem_mib * 2**20),
        cost_estimate=pl.CostEstimate(flops=flops, bytes_accessed=nbytes, transcendentals=0),
    )(*args)


def pack_kernel(tiles, out):
    parts = out.shape[0]
    width = tiles.shape[3] // parts
    for at, (a, b) in enumerate(OFF):
        t = tile_of(a, b)
        first, second = tiles[0, t], tiles[1, t]
        for d in range(parts):
            cols = slice(d * width, (d + 1) * width)
            out[d, at] = jnp.concatenate([first[:, cols], second[:, cols]], axis=1)


def own_kernel(tiles, coeffs, out):
    size = tiles.shape[3]
    rows = 2 * tiles.shape[2]
    for m in range(NB):
        lhs = jnp.concatenate([tiles[:, tile_of(a, m)].reshape(rows, size) for a in range(m + 1)], axis=0)
        part = jnp.dot(lhs, coeffs[m * size : (m + 1) * size], preferred_element_type=F32)
        part = part.reshape(m + 1, rows, part.shape[1])
        if m:
            out[:m] = out[:m] + part[:m]
        out[m] = part[m]


def lower_kernel(received, coeffs, own, out):
    size = received.shape[0] * received.shape[2]
    lanes = received.shape[3]
    half = lanes // 2
    occ = coeffs.shape[1]
    sums = [own[b] for b in range(NB)]
    for a in range(NB - 1):
        lhs = jnp.concatenate(
            [received[:, OFF_AT[a, b]].reshape(size, lanes) for b in range(a + 1, NB)], axis=1
        )
        part = lax.dot_general(
            lhs, coeffs[a * size : (a + 1) * size], (((0,), (0,)), ((), ())), preferred_element_type=F32
        )
        for b in range(a + 1, NB):
            at = (b - a - 1) * lanes
            sums[b] = sums[b] + part[at : at + lanes]
    for b in range(NB):
        both = sums[b].astype(BF16)
        rows = slice(b * half, (b + 1) * half)
        out[rows, :occ] = both[:half]
        out[rows, occ:] = both[half:]


def tiles_kernel(mine, own, sib, left, right, left_s, right_s, opp_a, opp_b, opp_as, opp_bs, out):
    width = mine.shape[0] // NB
    cols = mine[...]
    xs, cores = lax.axis_size("x"), lax.axis_size("core")
    x, core = lax.axis_index("x"), lax.axis_index("core")
    places = [
        lax.rem(x + dx, xs) * cores + lax.rem(core + dc, cores)
        for dx, dc in ((0, 0), (0, 1), (xs - 1, 0), (1, 0), (xs - 1, 1), (1, 1), (2, 0), (2, 1))
    ]

    def rows_of(piece, first, count, place):
        full = lax.dot_general(
            piece[...], cols, (((1,), (1,)), ((), ())), preferred_element_type=F32
        ).astype(BF16)
        high = out.shape[1]
        groups = width // high
        for k in range(count):
            a = first + k
            part = full[k * width : (k + 1) * width, a * width :]
            begin = tile_of(a, a) * width
            out[pl.ds(place * groups, groups), :, begin : begin + part.shape[1]] = part.reshape(
                groups, high, part.shape[1]
            )

    for at, piece in enumerate((own, sib, left, right, left_s, right_s)):
        rows_of(piece, 0, NB, places[at])
    rows_of(opp_a, 0, NB // 2, places[6])
    rows_of(opp_b, NB // 2, NB // 2, places[6])
    rows_of(opp_as, 0, NB // 2, places[7])
    rows_of(opp_bs, NB // 2, NB // 2, places[7])


def sum_kernel(received, out):
    total = received[0].astype(F32)
    for k in range(1, received.shape[0]):
        total = total + received[k].astype(F32)
    width = out.shape[2]
    for t in range(out.shape[0]):
        out[t] = total[:, t * width : (t + 1) * width]


def body(integrals, orbitals):
    slabs, tile_count, width, size = integrals.shape
    occ = orbitals.shape[1]
    xs, cores = lax.axis_size("x"), lax.axis_size("core")
    parts = xs * cores
    aux = lax.axis_size("z") * lax.axis_size("y")
    flops = 2 * slabs * width * size * occ

    packed = call(
        pack_kernel,
        jax.ShapeDtypeStruct((parts, len(OFF), width, slabs * width), BF16),
        (integrals,),
        0,
        2 * integrals.size * 2,
        12,
    )
    received = lax.all_to_all(packed, ("x", "core"), 0, 0)
    own = call(
        own_kernel,
        jax.ShapeDtypeStruct((NB, slabs * width, occ), F32),
        (integrals, orbitals),
        flops * tile_count,
        2 * integrals.size + 2 * orbitals.size,
        16,
    )
    half = call(
        lower_kernel,
        jax.ShapeDtypeStruct((NB * width, slabs * occ), BF16),
        (received, orbitals, own),
        flops * len(OFF),
        2 * received.size + 2 * orbitals.size,
        20,
    )

    up = [(i, (i + 1) % xs) for i in range(xs)]
    down = [(i, (i - 1) % xs) for i in range(xs)]
    swap = [(i, (i + 1) % cores) for i in range(cores)]
    mid = half.shape[0] // 2
    left = lax.ppermute(half, "x", up)
    right = lax.ppermute(half, "x", down)
    sib = lax.ppermute(half, "core", swap)
    opp_a = lax.ppermute(left[:mid], "x", up)
    opp_b = lax.ppermute(right[mid:], "x", down)
    left_s = lax.ppermute(left, "core", swap)
    right_s = lax.ppermute(right, "core", swap)
    opp_as = lax.ppermute(opp_a, "core", swap)
    opp_bs = lax.ppermute(opp_b, "core", swap)

    pieces = (half, half, sib, left, right, left_s, right_s, opp_a, opp_b, opp_as, opp_bs)
    partial = call(
        tiles_kernel,
        jax.ShapeDtypeStruct((aux, size // aux, tile_count * width), BF16),
        pieces,
        2 * size * NB * slabs * occ * NB * width,
        9 * 2 * half.size,
        20,
    )
    arrived = lax.all_to_all(partial, ("z", "y"), 0, 0)
    tiles = call(
        sum_kernel,
        jax.ShapeDtypeStruct((tile_count, size // aux, width), F32),
        (arrived,),
        arrived.size,
        2 * arrived.size,
        8,
    )
    return jnp.transpose(tiles, (1, 0, 2))


def solution(mesh):
    grid = Mesh(mesh.devices.reshape(8, 8, 4, 2), ("z", "y", "x", "core"))
    return jax.shard_map(
        body,
        mesh=grid,
        in_specs=(P(("z", "y"), None, ("x", "core"), None), P()),
        out_specs=P(("z", "y"), None, ("x", "core")),
        check_vma=False,
    )
```

```python
import jax
import jax.numpy as jnp
import numpy as np
from jax import lax
from jax.experimental import pallas as pl
from jax.experimental.pallas import tpu as pltpu
from jax.sharding import Mesh
from jax.sharding import PartitionSpec as P


NB = 6
AXES = ("z", "y", "x", "core")
F32 = jnp.float32
BF16 = jnp.bfloat16
VMEM = pl.BlockSpec(memory_space=pltpu.VMEM)
HBM = pl.BlockSpec(memory_space=pltpu.HBM)


def tile_of(a, b):
    return a * NB - a * (a - 1) // 2 + b - a


OFF = [(a, b) for a in range(NB) for b in range(a + 1, NB)]
OFF_AT = {pair: at for at, pair in enumerate(OFF)}


def call(kernel, out_shape, args, flops, nbytes, vmem_mib, **options):
    options.setdefault("in_specs", [VMEM] * len(args))
    options.setdefault("out_specs", jax.tree.map(lambda _: VMEM, out_shape))
    return pl.pallas_call(
        kernel,
        out_shape=out_shape,
        compiler_params=pltpu.CompilerParams(vmem_limit_bytes=vmem_mib * 2**20),
        cost_estimate=pl.CostEstimate(flops=flops, bytes_accessed=nbytes, transcendentals=0),
        **options,
    )(*args)


def pack_kernel(tiles, out):
    parts = out.shape[0]
    width = tiles.shape[3] // parts
    for at, (a, b) in enumerate(OFF):
        t = tile_of(a, b)
        first, second = tiles[0, t], tiles[1, t]
        for d in range(parts):
            cols = slice(d * width, (d + 1) * width)
            out[d, at] = jnp.concatenate([first[:, cols], second[:, cols]], axis=1)


def own_kernel(tiles, coeffs, out):
    size = tiles.shape[3]
    rows = 2 * tiles.shape[2]
    for m in range(NB):
        lhs = jnp.concatenate([tiles[:, tile_of(a, m)].reshape(rows, size) for a in range(m + 1)], axis=0)
        part = jnp.dot(lhs, coeffs[m * size : (m + 1) * size], preferred_element_type=F32)
        part = part.reshape(m + 1, rows, part.shape[1])
        if m:
            out[:m] = out[:m] + part[:m]
        out[m] = part[m]


def lower_kernel(received, coeffs_hbm, own_hbm, out, out_a, out_b, coeffs, own, sems):
    size = received.shape[0] * received.shape[2]
    lanes = received.shape[3]
    half = lanes // 2
    occ = coeffs.shape[1]
    copies = []
    for a in range(NB - 1):
        rows = pl.ds(a * size, size)
        copies.append(pltpu.make_async_copy(coeffs_hbm.at[rows], coeffs.at[rows], sems.at[a]))
    own_copy = pltpu.make_async_copy(own_hbm, own, sems.at[NB - 1])
    copies[0].start()
    own_copy.start()
    for copy in copies[1:]:
        copy.start()
    sums = [None] * NB
    for a in range(NB - 1):
        copies[a].wait()
        lhs = jnp.concatenate(
            [received[:, OFF_AT[a, b]].reshape(size, lanes) for b in range(a + 1, NB)], axis=1
        )
        part = lax.dot_general(
            lhs, coeffs[a * size : (a + 1) * size], (((0,), (0,)), ((), ())), preferred_element_type=F32
        )
        if a == 0:
            own_copy.wait()
            sums = [own[b] for b in range(NB)]
        for b in range(a + 1, NB):
            at = (b - a - 1) * lanes
            sums[b] = sums[b] + part[at : at + lanes]
    for b in range(NB):
        both = sums[b].astype(BF16)
        side = out_a if b < NB // 2 else out_b
        for ref, at in ((out, b), (side, b % (NB // 2))):
            ref[at * half : (at + 1) * half, :occ] = both[:half]
            ref[at * half : (at + 1) * half, occ:] = both[half:]


def tiles_kernel(pieces, mine, sib, out_mine, out_sib):
    width = mine.shape[0] // NB
    high = out_mine.shape[1]
    groups = width // high
    for cols, out in ((mine, out_mine), (sib, out_sib)):
        right = cols[...]
        for piece, first, count, place in pieces:
            full = lax.dot_general(
                piece[...], right, (((1,), (1,)), ((), ())), preferred_element_type=F32
            ).astype(BF16)
            for k in range(count):
                a = first + k
                part = full[k * width : (k + 1) * width, a * width :]
                begin = tile_of(a, a) * width
                out[place * groups : (place + 1) * groups, :, begin : begin + part.shape[1]] = part.reshape(
                    groups, high, part.shape[1]
                )


def near_kernel(own, left_a, left_b, right_a, right_b, sib, out_mine, out_sib):
    pieces = [(own, 0, NB, 0)]
    for place, (low, high) in ((1, (left_a, left_b)), (2, (right_a, right_b))):
        pieces += [(low, 0, NB // 2, place), (high, NB // 2, NB // 2, place)]
    tiles_kernel(pieces, own, sib, out_mine, out_sib)


def far_kernel(far_a, far_b, own, sib, out_mine, out_sib):
    pieces = [(far_a, 0, NB // 2, 0), (far_b, NB // 2, NB // 2, 0)]
    tiles_kernel(pieces, own, sib, out_mine, out_sib)


def gather_kernel(near, far, near_s, far_s, out):
    xs, cores = lax.axis_size("x"), lax.axis_size("core")
    zs, ys = lax.axis_size("z"), lax.axis_size("y")
    x, core = lax.axis_index("x"), lax.axis_index("core")
    for dc, sources in ((0, (near, far)), (1, (near_s, far_s))):
        for at, dx in enumerate((0, xs - 1, 1, 2)):
            source, first = (sources[0], at * ys) if at < 3 else (sources[1], 0)
            z = lax.rem(x + dx, xs) * cores + lax.rem(core + dc, cores)
            for y in range(ys):
                out[jnp.where(core == 0, z * ys + y, y * zs + z)] = source[first + y]


def sum_of(received):
    total = received[0].astype(F32)
    for k in range(1, received.shape[0]):
        total = total + received[k].astype(F32)
    return total


def sum_kernel(received, out):
    out[...] = sum_of(received)


def last_kernel(received, out):
    total = sum_of(received)
    width = out.shape[2]
    for t in range(out.shape[0]):
        out[t] = total[:, t * width : (t + 1) * width]


def body(integrals, orbitals):
    slabs, tile_count, width, size = integrals.shape
    occ = orbitals.shape[1]
    xs, cores, zs, ys = (lax.axis_size(name) for name in ("x", "core", "z", "y"))
    parts = xs * cores
    rows = size // (zs * ys)
    flops = 2 * slabs * width * size * occ

    lane_block = size // xs
    packed = call(
        pack_kernel,
        jax.ShapeDtypeStruct((parts, len(OFF), width, slabs * width), BF16),
        (integrals,),
        0,
        2 * integrals.size * 2,
        56,
        grid=(xs,),
        in_specs=[pl.BlockSpec((slabs, tile_count, width, lane_block), lambda i: (0, 0, 0, i))],
        out_specs=pl.BlockSpec((cores, len(OFF), width, slabs * width), lambda i: (i, 0, 0, 0)),
    )
    received = lax.all_to_all(packed, ("x", "core"), 0, 0)
    own = call(
        own_kernel,
        jax.ShapeDtypeStruct((NB, slabs * width, occ), F32),
        (integrals, orbitals),
        flops * tile_count,
        2 * integrals.size + 2 * orbitals.size,
        56,
    )
    share = jax.ShapeDtypeStruct((NB * width, slabs * occ), BF16)
    side = jax.ShapeDtypeStruct((NB // 2 * width, slabs * occ), BF16)
    half, half_a, half_b = call(
        lower_kernel,
        (share, side, side),
        (received, orbitals, own),
        flops * len(OFF),
        2 * received.size + 2 * orbitals.size,
        20,
        in_specs=[VMEM, HBM, HBM],
        scratch_shapes=[
            pltpu.VMEM(orbitals.shape, BF16),
            pltpu.VMEM(own.shape, F32),
            pltpu.SemaphoreType.DMA((NB,)),
        ],
    )

    up = [(i, (i + 1) % xs) for i in range(xs)]
    down = [(i, (i - 1) % xs) for i in range(xs)]
    swap = [(i, (i + 1) % cores) for i in range(cores)]
    left_a = lax.ppermute(half_a, "x", up)
    right_b = lax.ppermute(half_b, "x", down)
    left_b = lax.ppermute(half_b, "x", up)
    right_a = lax.ppermute(half_a, "x", down)
    far_a = lax.ppermute(left_a, "x", up)
    far_b = lax.ppermute(right_b, "x", down)
    sib = lax.ppermute(half, "core", swap)

    product = 2 * share.shape[0] ** 2 * share.shape[1]
    near_shape = jax.ShapeDtypeStruct((3 * ys, rows, tile_count * width), BF16)
    far_shape = jax.ShapeDtypeStruct((ys, rows, tile_count * width), BF16)
    near, near_s = call(
        near_kernel,
        (near_shape, near_shape),
        (half, left_a, left_b, right_a, right_b, sib),
        6 * product,
        8 * half.size,
        16,
    )
    near_s = lax.ppermute(near_s, "core", swap)
    far, far_s = call(
        far_kernel, (far_shape, far_shape), (far_a, far_b, half, sib), 2 * product, 6 * half.size, 12
    )
    far_s = lax.ppermute(far_s, "core", swap)
    partial = call(
        gather_kernel,
        jax.ShapeDtypeStruct((zs * ys, rows, tile_count * width), BF16),
        (near, far, near_s, far_s),
        0,
        8 * near.size,
        12,
    )

    at = np.arange(zs * ys * parts).reshape(zs, ys, xs, cores)
    along_z = [[at[:, y, x, c].tolist() for x in range(xs) for y in range(ys)] for c in range(2)]
    along_y = [[at[z, :, x, c].tolist() for x in range(xs) for z in range(zs)] for c in range(2)]
    arrived = lax.all_to_all(
        partial.reshape(zs, ys * rows, tile_count * width), AXES, 0, 0, axis_index_groups=along_z[0] + along_y[1]
    )
    summed = call(
        sum_kernel,
        jax.ShapeDtypeStruct(arrived.shape[1:], F32),
        (arrived,),
        arrived.size,
        2 * arrived.size,
        8,
    )
    arrived = lax.all_to_all(
        summed.reshape(ys, rows, tile_count * width), AXES, 0, 0, axis_index_groups=along_y[0] + along_z[1]
    )
    tiles = call(
        last_kernel,
        jax.ShapeDtypeStruct((tile_count, rows, width), F32),
        (arrived,),
        arrived.size,
        4 * arrived.size,
        8,
    )
    return jnp.transpose(tiles, (1, 0, 2))


def solution(mesh):
    grid = Mesh(mesh.devices.reshape(8, 8, 4, 2), AXES)
    return jax.shard_map(
        body,
        mesh=grid,
        in_specs=(P(("z", "y"), None, ("x", "core"), None), P()),
        out_specs=P(("z", "y"), None, ("x", "core")),
        check_vma=False,
    )
```

```python
import jax
import jax.numpy as jnp
import numpy as np
from jax import lax
from jax.experimental import pallas as pl
from jax.experimental.pallas import tpu as pltpu
from jax.sharding import Mesh
from jax.sharding import PartitionSpec as P


NB = 6
AXES = ("z", "y", "x", "core")
F32 = jnp.float32
BF16 = jnp.bfloat16
VMEM = pl.BlockSpec(memory_space=pltpu.VMEM)
ANY = pl.BlockSpec(memory_space=pl.ANY)


def tile_of(a, b):
    return a * NB - a * (a - 1) // 2 + b - a


OFF = [(a, b) for a in range(NB) for b in range(a + 1, NB)]
OFF_AT = {pair: at for at, pair in enumerate(OFF)}


def call(kernel, out_shape, args, flops, nbytes, vmem_mib, **options):
    options.setdefault("in_specs", [VMEM] * len(args))
    options.setdefault("out_specs", jax.tree.map(lambda _: VMEM, out_shape))
    return pl.pallas_call(
        kernel,
        out_shape=out_shape,
        compiler_params=pltpu.CompilerParams(vmem_limit_bytes=vmem_mib * 2**20),
        cost_estimate=pl.CostEstimate(flops=flops, bytes_accessed=nbytes, transcendentals=0),
        **options,
    )(*args)


def pack_kernel(tiles_hbm, out_hbm, tiles, out, sems):
    parts = out.shape[0]
    width = tiles.shape[3] // parts
    loads, stores = [], []
    for a in range(NB - 1):
        stored = pl.ds(tile_of(a, a + 1), NB - 1 - a)
        held = pl.ds(OFF_AT[a, a + 1], NB - 1 - a)
        loads.append(pltpu.make_async_copy(tiles_hbm.at[:, stored], tiles.at[:, held], sems.at[0, a]))
        stores.append(pltpu.make_async_copy(out.at[:, held], out_hbm.at[:, held], sems.at[1, a]))
    for load in loads:
        load.start()
    for at, (a, b) in enumerate(OFF):
        if b == a + 1:
            loads[a].wait()
        first, second = tiles[0, at], tiles[1, at]
        for d in range(parts):
            cols = slice(d * width, (d + 1) * width)
            out[d, at] = jnp.concatenate([first[:, cols], second[:, cols]], axis=1)
        if b == NB - 1:
            stores[a].start()
    for store in stores:
        store.wait()


def own_kernel(tiles, coeffs, out):
    size = tiles.shape[3]
    rows = 2 * tiles.shape[2]
    for m in range(NB):
        lhs = jnp.concatenate([tiles[:, tile_of(a, m)].reshape(rows, size) for a in range(m + 1)], axis=0)
        part = jnp.dot(lhs, coeffs[m * size : (m + 1) * size], preferred_element_type=F32)
        part = part.reshape(m + 1, rows, part.shape[1])
        if m:
            out[:m] = out[:m] + part[:m]
        out[m] = part[m]


def lower_kernel(received_hbm, coeffs_hbm, own_hbm, out, received, coeffs, own, sems):
    size = received.shape[0] * received.shape[2]
    lanes = received.shape[3]
    half = lanes // 2
    occ = coeffs.shape[1]
    loads = []
    for a in range(NB - 1):
        tiles = pl.ds(OFF_AT[a, a + 1], NB - 1 - a)
        rows = pl.ds(a * size, size)
        loads.append(
            (
                pltpu.make_async_copy(received_hbm.at[:, tiles], received.at[:, tiles], sems.at[0, a]),
                pltpu.make_async_copy(coeffs_hbm.at[rows], coeffs.at[rows], sems.at[1, a]),
            )
        )
    own_load = pltpu.make_async_copy(own_hbm, own, sems.at[0, NB - 1])
    order = list(range(NB - 1))
    for a in order:
        for load in loads[a]:
            load.start()
    own_load.start()
    sums = [None] * NB
    for a in order:
        for load in loads[a]:
            load.wait()
        lhs = jnp.concatenate(
            [received[:, OFF_AT[a, b]].reshape(size, lanes) for b in range(a + 1, NB)], axis=1
        )
        part = lax.dot_general(
            lhs, coeffs[a * size : (a + 1) * size], (((0,), (0,)), ((), ())), preferred_element_type=F32
        )
        for b in range(a + 1, NB):
            at = (b - a - 1) * lanes
            term = part[at : at + lanes]
            sums[b] = term if sums[b] is None else sums[b] + term
    own_load.wait()
    for b in range(NB):
        both = own[b] if sums[b] is None else sums[b] + own[b]
        both = both.astype(BF16)
        out[b * half : (b + 1) * half, :occ] = both[:half]
        out[b * half : (b + 1) * half, occ:] = both[half:]


def tiles_kernel(pieces, mine, sib, out_mine, out_sib):
    width = mine.shape[0] // NB
    high = out_mine.shape[1]
    groups = width // high
    for cols, out in ((mine, out_mine), (sib, out_sib)):
        right = cols[...]
        for place, piece in enumerate(pieces):
            full = lax.dot_general(
                piece[...], right, (((1,), (1,)), ((), ())), preferred_element_type=F32
            ).astype(BF16)
            for a in range(NB):
                part = full[a * width : (a + 1) * width, a * width :]
                begin = tile_of(a, a) * width
                out[place * groups : (place + 1) * groups, :, begin : begin + part.shape[1]] = part.reshape(
                    groups, high, part.shape[1]
                )


def near_kernel(own, first, second, sib, out_mine, out_sib):
    tiles_kernel((own, first, second), own, sib, out_mine, out_sib)


def far_kernel(far, own, sib, out_mine, out_sib):
    tiles_kernel((far,), own, sib, out_mine, out_sib)


def gather_kernel(near, far, near_s, far_s, out):
    cores = lax.axis_size("core")
    zs, ys = lax.axis_size("z"), lax.axis_size("y")
    x, core = lax.axis_index("x"), lax.axis_index("core")
    even = core == 0
    first, second = jnp.where(even, x ^ 1, x ^ 3), jnp.where(even, x ^ 3, x ^ 1)
    for places, source, parity in (
        ((x, first, second), near, core),
        ((x ^ 2,), far, core),
        ((x, second, first), near_s, 1 - core),
        ((x ^ 2,), far_s, 1 - core),
    ):
        for at, place in enumerate(places):
            z = place * cores + parity
            for y in range(ys):
                out[jnp.where(even, z * ys + y, y * zs + z)] = source[at * ys + y]


def sum_of(received):
    total = received[0].astype(F32)
    for k in range(1, received.shape[0]):
        total = total + received[k].astype(F32)
    return total


def sum_kernel(received, out):
    out[...] = sum_of(received)


def last_kernel(received, out):
    total = sum_of(received)
    width = out.shape[2]
    for t in range(out.shape[0]):
        out[t] = total[:, t * width : (t + 1) * width]


def body(integrals, orbitals):
    slabs, tile_count, width, size = integrals.shape
    occ = orbitals.shape[1]
    xs, cores, zs, ys = (lax.axis_size(name) for name in ("x", "core", "z", "y"))
    parts = xs * cores
    rows = size // (zs * ys)
    flops = 2 * slabs * width * size * occ

    packed = call(
        pack_kernel,
        jax.ShapeDtypeStruct((parts, len(OFF), width, slabs * width), BF16),
        (integrals,),
        0,
        2 * integrals.size * 2,
        63,
        in_specs=[ANY],
        out_specs=ANY,
        scratch_shapes=[
            pltpu.VMEM((slabs, len(OFF), width, size), BF16),
            pltpu.VMEM((parts, len(OFF), width, slabs * width), BF16),
            pltpu.SemaphoreType.DMA((2, NB - 1)),
        ],
    )
    received = lax.all_to_all(packed, ("x", "core"), 0, 0)
    own = call(
        own_kernel,
        jax.ShapeDtypeStruct((NB, slabs * width, occ), F32),
        (integrals, orbitals),
        flops * tile_count,
        2 * integrals.size + 2 * orbitals.size,
        63,
    )
    half = call(
        lower_kernel,
        jax.ShapeDtypeStruct((NB * width, slabs * occ), BF16),
        (received, orbitals, own),
        flops * len(OFF),
        2 * received.size + 2 * orbitals.size,
        63,
        in_specs=[ANY] * 3,
        scratch_shapes=[
            pltpu.VMEM(received.shape, BF16),
            pltpu.VMEM(orbitals.shape, BF16),
            pltpu.VMEM(own.shape, F32),
            pltpu.SemaphoreType.DMA((2, NB)),
        ],
    )

    def exchange(array, turn):
        pairs = [((x, c), (x ^ (3 if (c + turn) % 2 else 1), c)) for x in range(xs) for c in range(cores)]
        return lax.ppermute(array, ("x", "core"), [(a * cores + c, b * cores + d) for (a, c), (b, d) in pairs])

    swap = [(i, (i + 1) % cores) for i in range(cores)]
    first = exchange(half, 0)
    second = exchange(half, 1)
    sib = lax.ppermute(half, "core", swap)
    far = exchange(first, 1)

    product = 2 * half.shape[0] ** 2 * half.shape[1]
    near_shape = jax.ShapeDtypeStruct((3 * ys, rows, tile_count * width), BF16)
    far_shape = jax.ShapeDtypeStruct((ys, rows, tile_count * width), BF16)
    near, near_s = call(
        near_kernel,
        (near_shape, near_shape),
        (half, first, second, sib),
        6 * product,
        8 * half.size,
        16,
    )
    near_s = lax.ppermute(near_s, "core", swap)
    far, far_s = call(far_kernel, (far_shape, far_shape), (far, half, sib), 2 * product, 6 * half.size, 12)
    far_s = lax.ppermute(far_s, "core", swap)
    partial = call(
        gather_kernel,
        jax.ShapeDtypeStruct((zs * ys, rows, tile_count * width), BF16),
        (near, far, near_s, far_s),
        0,
        8 * near.size,
        12,
    )

    at = np.arange(zs * ys * parts).reshape(zs, ys, xs, cores)
    along_z = [[at[:, y, x, c].tolist() for x in range(xs) for y in range(ys)] for c in range(2)]
    along_y = [[at[z, :, x, c].tolist() for x in range(xs) for z in range(zs)] for c in range(2)]
    arrived = lax.all_to_all(
        partial.reshape(zs, ys * rows, tile_count * width), AXES, 0, 0, axis_index_groups=along_z[0] + along_y[1]
    )
    summed = call(
        sum_kernel,
        jax.ShapeDtypeStruct(arrived.shape[1:], F32),
        (arrived,),
        arrived.size,
        2 * arrived.size,
        8,
    )
    arrived = lax.all_to_all(
        summed.reshape(ys, rows, tile_count * width), AXES, 0, 0, axis_index_groups=along_y[0] + along_z[1]
    )
    tiles = call(
        last_kernel,
        jax.ShapeDtypeStruct((tile_count, rows, width), F32),
        (arrived,),
        arrived.size,
        4 * arrived.size,
        8,
    )
    return jnp.transpose(tiles, (1, 0, 2))


def solution(mesh):
    grid = Mesh(mesh.devices.reshape(8, 8, 4, 2), AXES)
    return jax.shard_map(
        body,
        mesh=grid,
        in_specs=(P(("z", "y"), None, ("x", "core"), None), P()),
        out_specs=P(("z", "y"), None, ("x", "core")),
        check_vma=False,
    )
```

```python
import jax
import jax.numpy as jnp
import numpy as np
from jax import lax
from jax.experimental import pallas as pl
from jax.experimental.pallas import tpu as pltpu
from jax.sharding import Mesh
from jax.sharding import PartitionSpec as P


NB = 6
AXES = ("z", "y", "x", "core")
F32 = jnp.float32
BF16 = jnp.bfloat16
VMEM = pl.BlockSpec(memory_space=pltpu.VMEM)
ANY = pl.BlockSpec(memory_space=pl.ANY)


def tile_of(a, b):
    return a * NB - a * (a - 1) // 2 + b - a


OFF = [(a, b) for a in range(NB) for b in range(a + 1, NB)]
OFF_AT = {pair: at for at, pair in enumerate(OFF)}


def call(kernel, out_shape, args, flops, nbytes, vmem_mib, **options):
    options.setdefault("in_specs", [VMEM] * len(args))
    options.setdefault("out_specs", jax.tree.map(lambda _: VMEM, out_shape))
    return pl.pallas_call(
        kernel,
        out_shape=out_shape,
        compiler_params=pltpu.CompilerParams(vmem_limit_bytes=vmem_mib * 2**20),
        cost_estimate=pl.CostEstimate(flops=flops, bytes_accessed=nbytes, transcendentals=0),
        **options,
    )(*args)


def pack_kernel(tiles_hbm, out_hbm, tiles, out, sems):
    parts = out.shape[0]
    width = tiles.shape[3] // parts
    loads, stores = [], []
    for a in range(NB - 1):
        stored = pl.ds(tile_of(a, a + 1), NB - 1 - a)
        held = pl.ds(OFF_AT[a, a + 1], NB - 1 - a)
        loads.append(pltpu.make_async_copy(tiles_hbm.at[:, stored], tiles.at[:, held], sems.at[0, a]))
        stores.append(pltpu.make_async_copy(out.at[:, held], out_hbm.at[:, held], sems.at[1, a]))
    for load in loads:
        load.start()
    for at, (a, b) in enumerate(OFF):
        if b == a + 1:
            loads[a].wait()
        first, second = tiles[0, at], tiles[1, at]
        for d in range(parts):
            cols = slice(d * width, (d + 1) * width)
            out[d, at] = jnp.concatenate([first[:, cols], second[:, cols]], axis=1)
        if b == NB - 1:
            stores[a].start()
    for store in stores:
        store.wait()


def own_kernel(tiles, coeffs, out):
    size = tiles.shape[3]
    rows = 2 * tiles.shape[2]
    for m in range(NB):
        lhs = jnp.concatenate([tiles[:, tile_of(a, m)].reshape(rows, size) for a in range(m + 1)], axis=0)
        part = jnp.dot(lhs, coeffs[m * size : (m + 1) * size], preferred_element_type=F32)
        part = part.reshape(m + 1, rows, part.shape[1])
        if m:
            out[:m] = out[:m] + part[:m]
        out[m] = part[m]


def lower_kernel(received_hbm, coeffs_hbm, own_hbm, out, out_a, out_b, received, coeffs, own, sems):
    size = received.shape[0] * received.shape[2]
    lanes = received.shape[3]
    half = lanes // 2
    occ = coeffs.shape[1]
    loads = []
    for a in range(NB - 1):
        tiles = pl.ds(OFF_AT[a, a + 1], NB - 1 - a)
        rows = pl.ds(a * size, size)
        loads.append(
            (
                pltpu.make_async_copy(received_hbm.at[:, tiles], received.at[:, tiles], sems.at[0, a]),
                pltpu.make_async_copy(coeffs_hbm.at[rows], coeffs.at[rows], sems.at[1, a]),
            )
        )
    loads.append((pltpu.make_async_copy(own_hbm, own, sems.at[0, NB - 1]),))
    for load in loads[0] + loads[1]:
        load.start()
    sums = [None] * NB
    for a in range(NB - 1):
        for load in loads[a]:
            load.wait()
        if a + 2 < NB:
            for load in loads[a + 2]:
                load.start()
        lhs = jnp.concatenate(
            [received[:, OFF_AT[a, b]].reshape(size, lanes) for b in range(a + 1, NB)], axis=1
        )
        part = lax.dot_general(
            lhs, coeffs[a * size : (a + 1) * size], (((0,), (0,)), ((), ())), preferred_element_type=F32
        )
        for b in range(a + 1, NB):
            at = (b - a - 1) * lanes
            term = part[at : at + lanes]
            sums[b] = term if sums[b] is None else sums[b] + term
    loads[NB - 1][0].wait()
    for b in range(NB):
        both = own[b] if sums[b] is None else sums[b] + own[b]
        both = both.astype(BF16)
        for ref, at in ((out, b), (out_a if b < NB // 2 else out_b, b % (NB // 2))):
            ref[at * half : (at + 1) * half, :occ] = both[:half]
            ref[at * half : (at + 1) * half, occ:] = both[half:]


def tiles_kernel(pieces, mine, sib, out_mine, out_sib):
    width = mine.shape[0] // NB
    high = out_mine.shape[1]
    groups = width // high
    for cols, out in ((mine, out_mine), (sib, out_sib)):
        right = cols[...]
        for place, piece in enumerate(pieces):
            a = 0
            for part in piece:
                full = lax.dot_general(
                    part[...], right, (((1,), (1,)), ((), ())), preferred_element_type=F32
                ).astype(BF16)
                for k in range(part.shape[0] // width):
                    strip = full[k * width : (k + 1) * width, a * width :]
                    begin = tile_of(a, a) * width
                    out[place * groups : (place + 1) * groups, :, begin : begin + strip.shape[1]] = strip.reshape(
                        groups, high, strip.shape[1]
                    )
                    a += 1


def near_kernel(own, first_a, first_b, second, sib, out_mine, out_sib):
    tiles_kernel(((own,), (first_a, first_b), (second,)), own, sib, out_mine, out_sib)


def far_kernel(far_a, far_b, own, sib, out_mine, out_sib):
    tiles_kernel(((far_a, far_b),), own, sib, out_mine, out_sib)


def gather_kernel(near, far, near_s, far_s, out):
    cores = lax.axis_size("core")
    zs, ys = lax.axis_size("z"), lax.axis_size("y")
    x, core = lax.axis_index("x"), lax.axis_index("core")
    even = core == 0
    first, second = jnp.where(even, x ^ 1, x ^ 3), jnp.where(even, x ^ 3, x ^ 1)
    for places, source, parity in (
        ((x, first, second), near, core),
        ((x ^ 2,), far, core),
        ((x, second, first), near_s, 1 - core),
        ((x ^ 2,), far_s, 1 - core),
    ):
        for at, place in enumerate(places):
            z = place * cores + parity
            for y in range(ys):
                out[jnp.where(even, z * ys + y, y * zs + z)] = source[at * ys + y]


def sum_of(received):
    total = received[0].astype(F32)
    for k in range(1, received.shape[0]):
        total = total + received[k].astype(F32)
    return total


def sum_kernel(received, out):
    out[...] = sum_of(received)


def last_kernel(received, out):
    total = sum_of(received)
    width = out.shape[2]
    for t in range(out.shape[0]):
        out[t] = total[:, t * width : (t + 1) * width]


def body(integrals, orbitals):
    slabs, tile_count, width, size = integrals.shape
    occ = orbitals.shape[1]
    xs, cores, zs, ys = (lax.axis_size(name) for name in ("x", "core", "z", "y"))
    parts = xs * cores
    rows = size // (zs * ys)
    flops = 2 * slabs * width * size * occ

    packed = call(
        pack_kernel,
        jax.ShapeDtypeStruct((parts, len(OFF), width, slabs * width), BF16),
        (integrals,),
        0,
        2 * integrals.size * 2,
        63,
        in_specs=[ANY],
        out_specs=ANY,
        scratch_shapes=[
            pltpu.VMEM((slabs, len(OFF), width, size), BF16),
            pltpu.VMEM((parts, len(OFF), width, slabs * width), BF16),
            pltpu.SemaphoreType.DMA((2, NB - 1)),
        ],
    )
    received = lax.all_to_all(packed, ("x", "core"), 0, 0)
    own = call(
        own_kernel,
        jax.ShapeDtypeStruct((NB, slabs * width, occ), F32),
        (integrals, orbitals),
        flops * tile_count,
        2 * integrals.size + 2 * orbitals.size,
        63,
    )
    whole = jax.ShapeDtypeStruct((NB * width, slabs * occ), BF16)
    side = jax.ShapeDtypeStruct((NB // 2 * width, slabs * occ), BF16)
    in_hbm = lambda array: pltpu.with_memory_space_constraint(array, pltpu.HBM)
    half, half_a, half_b = call(
        lower_kernel,
        (whole, side, side),
        (in_hbm(received), in_hbm(orbitals), in_hbm(own)),
        flops * len(OFF),
        2 * received.size + 2 * orbitals.size,
        20,
        in_specs=[ANY] * 3,
        scratch_shapes=[
            pltpu.VMEM(received.shape, BF16),
            pltpu.VMEM(orbitals.shape, BF16),
            pltpu.VMEM(own.shape, F32),
            pltpu.SemaphoreType.DMA((2, NB)),
        ],
    )

    def exchange(array, turn):
        pairs = [((x, c), (x ^ (3 if (c + turn) % 2 else 1), c)) for x in range(xs) for c in range(cores)]
        return lax.ppermute(array, ("x", "core"), [(a * cores + c, b * cores + d) for (a, c), (b, d) in pairs])

    swap = [(i, (i + 1) % cores) for i in range(cores)]
    first_a = exchange(half_a, 0)
    first_b = exchange(half_b, 0)
    second = exchange(half, 1)
    far_a = exchange(first_a, 1)
    sib = lax.ppermute(half, "core", swap)
    far_b = exchange(first_b, 1)

    product = 2 * half.shape[0] ** 2 * half.shape[1]
    near_shape = jax.ShapeDtypeStruct((3 * ys, rows, tile_count * width), BF16)
    far_shape = jax.ShapeDtypeStruct((ys, rows, tile_count * width), BF16)
    near, near_s = call(
        near_kernel,
        (near_shape, near_shape),
        (half, first_a, first_b, second, sib),
        6 * product,
        8 * half.size,
        16,
    )
    near_s = lax.ppermute(near_s, "core", swap)
    far, far_s = call(far_kernel, (far_shape, far_shape), (far_a, far_b, half, sib), 2 * product, 6 * half.size, 12)
    far_s = lax.ppermute(far_s, "core", swap)
    partial = call(
        gather_kernel,
        jax.ShapeDtypeStruct((zs * ys, rows, tile_count * width), BF16),
        (near, far, near_s, far_s),
        0,
        8 * near.size,
        12,
    )

    at = np.arange(zs * ys * parts).reshape(zs, ys, xs, cores)
    along_z = [[at[:, y, x, c].tolist() for x in range(xs) for y in range(ys)] for c in range(2)]
    along_y = [[at[z, :, x, c].tolist() for x in range(xs) for z in range(zs)] for c in range(2)]
    arrived = lax.all_to_all(
        partial.reshape(zs, ys * rows, tile_count * width), AXES, 0, 0, axis_index_groups=along_z[0] + along_y[1]
    )
    summed = call(
        sum_kernel,
        jax.ShapeDtypeStruct(arrived.shape[1:], F32),
        (arrived,),
        arrived.size,
        2 * arrived.size,
        8,
    )
    arrived = lax.all_to_all(
        summed.reshape(ys, rows, tile_count * width), AXES, 0, 0, axis_index_groups=along_y[0] + along_z[1]
    )
    tiles = call(
        last_kernel,
        jax.ShapeDtypeStruct((tile_count, rows, width), F32),
        (arrived,),
        arrived.size,
        4 * arrived.size,
        8,
    )
    return jnp.transpose(tiles, (1, 0, 2))


def solution(mesh):
    grid = Mesh(mesh.devices.reshape(8, 8, 4, 2), AXES)
    return jax.shard_map(
        body,
        mesh=grid,
        in_specs=(P(("z", "y"), None, ("x", "core"), None), P()),
        out_specs=P(("z", "y"), None, ("x", "core")),
        check_vma=False,
    )
```

```python
import jax
import jax.numpy as jnp
import numpy as np
from jax import lax
from jax.experimental import pallas as pl
from jax.experimental.pallas import tpu as pltpu
from jax.sharding import Mesh
from jax.sharding import PartitionSpec as P


NB = 6
AXES = ("z", "y", "x", "core")
F32 = jnp.float32
BF16 = jnp.bfloat16
VMEM = pl.BlockSpec(memory_space=pltpu.VMEM)
ANY = pl.BlockSpec(memory_space=pl.ANY)


def tile_of(a, b):
    return a * NB - a * (a - 1) // 2 + b - a


CUT = 4
OFF = [(a, b) for b in range(NB) for a in range(b)]
OFF_AT = {pair: at for at, pair in enumerate(OFF)}


def call(kernel, out_shape, args, flops, nbytes, vmem_mib, **options):
    options.setdefault("in_specs", [VMEM] * len(args))
    options.setdefault("out_specs", jax.tree.map(lambda _: VMEM, out_shape))
    return pl.pallas_call(
        kernel,
        out_shape=out_shape,
        compiler_params=pltpu.CompilerParams(vmem_limit_bytes=vmem_mib * 2**20),
        cost_estimate=pl.CostEstimate(flops=flops, bytes_accessed=nbytes, transcendentals=0),
        **options,
    )(*args)


def pack_kernel(tiles_hbm, out_hbm, tiles, out, sems):
    parts = out.shape[0]
    width = tiles.shape[3] // parts
    loads, stores = [], []
    for a in range(NB - 1):
        stored = pl.ds(tile_of(a, a + 1), NB - 1 - a)
        held = pl.ds(tile_of(a, a + 1) - a - 1, NB - 1 - a)
        loads.append(pltpu.make_async_copy(tiles_hbm.at[:, stored], tiles.at[:, held], sems.at[0, a]))
    for b in range(1, NB):
        ready = pl.ds(OFF_AT[0, b], b)
        stores.append(pltpu.make_async_copy(out.at[:, ready], out_hbm.at[:, ready], sems.at[1, b - 1]))
    for load in loads:
        load.start()
    for at, (a, b) in enumerate(OFF):
        if a == b - 1:
            loads[a].wait()
        first, second = (tiles[slab, tile_of(a, b) - a - 1] for slab in range(2))
        for d in range(parts):
            cols = slice(d * width, (d + 1) * width)
            out[d, at] = jnp.concatenate([first[:, cols], second[:, cols]], axis=1)
        if a == b - 1:
            stores[a].start()
    for store in stores:
        store.wait()


def own_kernel(tiles, coeffs, out):
    size = tiles.shape[3]
    rows = 2 * tiles.shape[2]
    for m in range(NB):
        lhs = jnp.concatenate([tiles[:, tile_of(a, m)].reshape(rows, size) for a in range(m + 1)], axis=0)
        part = jnp.dot(lhs, coeffs[m * size : (m + 1) * size], preferred_element_type=F32)
        part = part.reshape(m + 1, rows, part.shape[1])
        if m:
            out[:m] = out[:m] + part[:m]
        out[m] = part[m]


def lower_part(cols, received_hbm, coeffs_hbm, own_hbm, received, coeffs, own, sems):
    size = received.shape[0] * received.shape[2]
    lanes = received.shape[3]
    last = cols[-1]
    begin = OFF_AT[0, cols[0]] if cols[0] else 0
    count = OFF_AT[last - 1, last] + 1 - begin
    loads = [pltpu.make_async_copy(received_hbm.at[:, pl.ds(begin, count)], received, sems.at[0])]
    for a in range(last):
        rows = pl.ds(a * size, size)
        loads.append(pltpu.make_async_copy(coeffs_hbm.at[rows], coeffs.at[rows], sems.at[a + 1]))
    loads.append(pltpu.make_async_copy(own_hbm.at[pl.ds(cols[0], len(cols))], own, sems.at[last + 1]))
    for load in loads:
        load.start()
    loads[0].wait()
    sums = {b: None for b in cols}
    for a in range(last):
        loads[a + 1].wait()
        fed = [b for b in cols if b > a]
        lhs = jnp.concatenate(
            [received[:, OFF_AT[a, b] - begin].reshape(size, lanes) for b in fed], axis=1
        )
        part = lax.dot_general(
            lhs, coeffs[a * size : (a + 1) * size], (((0,), (0,)), ((), ())), preferred_element_type=F32
        )
        for at, b in enumerate(fed):
            term = part[at * lanes : (at + 1) * lanes]
            sums[b] = term if sums[b] is None else sums[b] + term
    loads[-1].wait()
    both = [own[at] if sums[b] is None else sums[b] + own[at] for at, b in enumerate(cols)]
    return [value.astype(BF16) for value in both]


def put_rows(values, out, begin):
    half, occ = values[0].shape[0] // 2, values[0].shape[1]
    for at, value in enumerate(values):
        rows = slice(begin + at * half, begin + (at + 1) * half)
        out[rows, :occ] = value[:half]
        out[rows, occ:] = value[half:]


def lower_a_kernel(received_hbm, coeffs_hbm, own_hbm, out_a, *scratch):
    put_rows(lower_part(range(CUT), received_hbm, coeffs_hbm, own_hbm, *scratch), out_a, 0)


def lower_b_kernel(received_hbm, coeffs_hbm, own_hbm, half_a, out, out_b, *scratch):
    values = lower_part(range(CUT, NB), received_hbm, coeffs_hbm, own_hbm, *scratch)
    put_rows(values, out_b, 0)
    out[: half_a.shape[0]] = half_a[...]
    put_rows(values, out, half_a.shape[0])


def tiles_kernel(pieces, mine, sib, out_mine, out_sib, base=0):
    width = mine.shape[0] // NB
    high = out_mine.shape[1]
    groups = width // high
    for cols, out in ((sib, out_sib), (mine, out_mine)):
        right = cols[...]
        for place, piece in enumerate(pieces):
            for first, part in piece:
                full = lax.dot_general(
                    part[...], right, (((1,), (1,)), ((), ())), preferred_element_type=F32
                ).astype(BF16)
                for k in range(part.shape[0] // width):
                    a = first + k
                    strip = full[k * width : (k + 1) * width, a * width :]
                    begin = tile_of(a, a) * width - base
                    out[place * groups : (place + 1) * groups, :, begin : begin + strip.shape[1]] = strip.reshape(
                        groups, high, strip.shape[1]
                    )


def near_kernel(own, first_a, first_b, second, sib, out_mine, out_sib):
    pieces = ([(0, own)], [(0, first_a), (CUT, first_b)], [(0, second)])
    tiles_kernel(pieces, own, sib, out_mine, out_sib)


def far_a_kernel(far_a, own, sib, out_mine, out_sib):
    tiles_kernel(([(0, far_a)],), own, sib, out_mine, out_sib)


def far_b_kernel(far_b, own, sib, out_mine, out_sib):
    base = tile_of(CUT, CUT) * own.shape[0] // NB
    tiles_kernel(([(CUT, far_b)],), own, sib, out_mine, out_sib, base)


def gather_kernel(near, far_a, far_b, near_s, far_as, far_bs, out):
    cores = lax.axis_size("core")
    zs, ys = lax.axis_size("z"), lax.axis_size("y")
    x, core = lax.axis_index("x"), lax.axis_index("core")
    even = core == 0
    first, second = jnp.where(even, x ^ 1, x ^ 3), jnp.where(even, x ^ 3, x ^ 1)
    cut = far_a.shape[2]
    for places, parity, close, low, high in (
        ((x, first, second, x ^ 2), core, near, far_a, far_b),
        ((x, second, first, x ^ 2), 1 - core, near_s, far_as, far_bs),
    ):
        for at, place in enumerate(places):
            z = place * cores + parity
            for y in range(ys):
                to = jnp.where(even, z * ys + y, y * zs + z)
                if at < 3:
                    out[to] = close[at * ys + y]
                else:
                    out[to, :, :cut] = low[y]
                    out[to, :, cut:] = high[y]


def sum_of(received):
    total = received[0].astype(F32)
    for k in range(1, received.shape[0]):
        total = total + received[k].astype(F32)
    return total


def sum_kernel(received, out):
    out[...] = sum_of(received).astype(out.dtype)


def last_kernel(received, out):
    total = sum_of(received)
    width = out.shape[2]
    for t in range(out.shape[0]):
        out[t] = total[:, t * width : (t + 1) * width]


def body(integrals, orbitals):
    slabs, tile_count, width, size = integrals.shape
    occ = orbitals.shape[1]
    xs, cores, zs, ys = (lax.axis_size(name) for name in ("x", "core", "z", "y"))
    parts = xs * cores
    rows = size // (zs * ys)
    flops = 2 * slabs * width * size * occ

    packed = call(
        pack_kernel,
        jax.ShapeDtypeStruct((parts, len(OFF), width, slabs * width), BF16),
        (integrals,),
        0,
        2 * integrals.size * 2,
        63,
        in_specs=[ANY],
        out_specs=ANY,
        scratch_shapes=[
            pltpu.VMEM((slabs, len(OFF), width, size), BF16),
            pltpu.VMEM((parts, len(OFF), width, slabs * width), BF16),
            pltpu.SemaphoreType.DMA((2, NB - 1)),
        ],
    )
    received = lax.all_to_all(packed, ("x", "core"), 0, 0)
    own = call(
        own_kernel,
        jax.ShapeDtypeStruct((NB, slabs * width, occ), F32),
        (integrals, orbitals),
        flops * tile_count,
        2 * integrals.size + 2 * orbitals.size,
        63,
    )
    low = jax.ShapeDtypeStruct((CUT * width, slabs * occ), BF16)
    high = jax.ShapeDtypeStruct(((NB - CUT) * width, slabs * occ), BF16)
    whole = jax.ShapeDtypeStruct((NB * width, slabs * occ), BF16)
    in_hbm = [pltpu.with_memory_space_constraint(array, pltpu.HBM) for array in (received, orbitals, own)]

    def lower(kernel, out_shape, args, cols):
        tiles = sum(cols)
        return call(
            kernel,
            out_shape,
            (*in_hbm, *args),
            flops * tiles,
            2 * tiles * parts * width * slabs * width + 2 * orbitals.size,
            20,
            in_specs=[ANY] * 3 + [VMEM] * len(args),
            scratch_shapes=[
                pltpu.VMEM((parts, tiles, width, slabs * width), BF16),
                pltpu.VMEM((cols[-1] * size, occ), BF16),
                pltpu.VMEM((len(cols), slabs * width, occ), F32),
                pltpu.SemaphoreType.DMA((cols[-1] + 2,)),
            ],
        )

    def exchange(array, turn):
        pairs = [((x, c), (x ^ (3 if (c + turn) % 2 else 1), c)) for x in range(xs) for c in range(cores)]
        return lax.ppermute(array, ("x", "core"), [(a * cores + c, b * cores + d) for (a, c), (b, d) in pairs])

    swap = [(i, (i + 1) % cores) for i in range(cores)]
    half_a = lower(lower_a_kernel, low, (), range(CUT))
    first_a = exchange(half_a, 0)
    half, half_b = lower(lower_b_kernel, (whole, high), (half_a,), range(CUT, NB))
    first_b = exchange(half_b, 0)
    second = exchange(half, 1)
    far_a = exchange(first_a, 1)
    sib = lax.ppermute(half, "core", swap)
    far_b = exchange(first_b, 1)

    product = 2 * half.shape[0] ** 2 * half.shape[1]
    cut = tile_of(CUT, CUT) * width
    near_shape = jax.ShapeDtypeStruct((3 * ys, rows, tile_count * width), BF16)
    low_shape = jax.ShapeDtypeStruct((ys, rows, cut), BF16)
    high_shape = jax.ShapeDtypeStruct((ys, rows, tile_count * width - cut), BF16)
    near, near_s = call(
        near_kernel,
        (near_shape, near_shape),
        (half, first_a, first_b, second, sib),
        6 * product,
        8 * half.size,
        16,
    )
    near_s = lax.ppermute(near_s, "core", swap)
    far_a, far_as = call(far_a_kernel, (low_shape, low_shape), (far_a, half, sib), 2 * product, 6 * half.size, 12)
    far_as = lax.ppermute(far_as, "core", swap)
    far_b, far_bs = call(
        far_b_kernel, (high_shape, high_shape), (far_b, half, sib), product, 6 * half.size, 12
    )
    far_bs = lax.ppermute(far_bs, "core", swap)
    partial = call(
        gather_kernel,
        jax.ShapeDtypeStruct((zs * ys, rows, tile_count * width), BF16),
        (near, far_a, far_b, near_s, far_as, far_bs),
        0,
        8 * near.size,
        12,
    )

    at = np.arange(zs * ys * parts).reshape(zs, ys, xs, cores)
    along_z = [[at[:, y, x, c].tolist() for x in range(xs) for y in range(ys)] for c in range(2)]
    along_y = [[at[z, :, x, c].tolist() for x in range(xs) for z in range(zs)] for c in range(2)]
    arrived = lax.all_to_all(
        partial.reshape(zs, ys * rows, tile_count * width), AXES, 0, 0, axis_index_groups=along_z[0] + along_y[1]
    )
    summed = call(
        sum_kernel,
        jax.ShapeDtypeStruct(arrived.shape[1:], BF16),
        (arrived,),
        arrived.size,
        2 * arrived.size,
        8,
    )
    arrived = lax.all_to_all(
        summed.reshape(ys, rows, tile_count * width), AXES, 0, 0, axis_index_groups=along_y[0] + along_z[1]
    )
    tiles = call(
        last_kernel,
        jax.ShapeDtypeStruct((tile_count, rows, width), F32),
        (arrived,),
        arrived.size,
        4 * arrived.size,
        8,
    )
    return jnp.transpose(tiles, (1, 0, 2))


def solution(mesh):
    grid = Mesh(mesh.devices.reshape(8, 8, 4, 2), AXES)
    return jax.shard_map(
        body,
        mesh=grid,
        in_specs=(P(("z", "y"), None, ("x", "core"), None), P()),
        out_specs=P(("z", "y"), None, ("x", "core")),
        check_vma=False,
    )
```

```python
import jax
import jax.numpy as jnp
import numpy as np
from jax import lax
from jax.experimental import pallas as pl
from jax.experimental.pallas import tpu as pltpu
from jax.sharding import Mesh
from jax.sharding import PartitionSpec as P


NB = 6
AXES = ("z", "y", "x", "core")
F32 = jnp.float32
BF16 = jnp.bfloat16
VMEM = pl.BlockSpec(memory_space=pltpu.VMEM)
ANY = pl.BlockSpec(memory_space=pl.ANY)


def tile_of(a, b):
    return a * NB - a * (a - 1) // 2 + b - a


OFF = [(a, b) for a in range(NB) for b in range(a + 1, NB)]
OFF_AT = {pair: at for at, pair in enumerate(OFF)}


def call(kernel, out_shape, args, flops, nbytes, vmem_mib, **options):
    options.setdefault("in_specs", [VMEM] * len(args))
    options.setdefault("out_specs", jax.tree.map(lambda _: VMEM, out_shape))
    return pl.pallas_call(
        kernel,
        out_shape=out_shape,
        compiler_params=pltpu.CompilerParams(vmem_limit_bytes=vmem_mib * 2**20),
        cost_estimate=pl.CostEstimate(flops=flops, bytes_accessed=nbytes, transcendentals=0),
        **options,
    )(*args)


def pack_kernel(tiles_hbm, out_hbm, tiles, out, sems):
    parts = out.shape[0]
    width = tiles.shape[3] // parts
    loads, stores = [], []
    for a in range(NB - 1):
        stored = pl.ds(tile_of(a, a + 1), NB - 1 - a)
        held = pl.ds(OFF_AT[a, a + 1], NB - 1 - a)
        loads.append(pltpu.make_async_copy(tiles_hbm.at[:, stored], tiles.at[:, held], sems.at[0, a]))
        stores.append(pltpu.make_async_copy(out.at[:, held], out_hbm.at[:, held], sems.at[1, a]))
    for load in loads:
        load.start()
    for at, (a, b) in enumerate(OFF):
        if b == a + 1:
            loads[a].wait()
        first, second = tiles[0, at], tiles[1, at]
        for d in range(parts):
            cols = slice(d * width, (d + 1) * width)
            out[d, at] = jnp.concatenate([first[:, cols], second[:, cols]], axis=1)
        if b == NB - 1:
            stores[a].start()
    for store in stores:
        store.wait()


def own_kernel(tiles, coeffs, out):
    size = tiles.shape[3]
    rows = 2 * tiles.shape[2]
    for m in range(NB):
        lhs = jnp.concatenate([tiles[:, tile_of(a, m)].reshape(rows, size) for a in range(m + 1)], axis=0)
        part = jnp.dot(lhs, coeffs[m * size : (m + 1) * size], preferred_element_type=F32)
        part = part.reshape(m + 1, rows, part.shape[1])
        if m:
            out[:m] = out[:m] + part[:m]
        out[m] = part[m]


def lower_kernel(received_hbm, coeffs_hbm, own_hbm, out, received, coeffs, own, sems):
    size = received.shape[0] * received.shape[2]
    lanes = received.shape[3]
    half = lanes // 2
    occ = coeffs.shape[1]
    loads = []
    for a in range(NB - 1):
        tiles = pl.ds(OFF_AT[a, a + 1], NB - 1 - a)
        rows = pl.ds(a * size, size)
        loads.append(
            (
                pltpu.make_async_copy(received_hbm.at[:, tiles], received.at[:, tiles], sems.at[0, a]),
                pltpu.make_async_copy(coeffs_hbm.at[rows], coeffs.at[rows], sems.at[1, a]),
            )
        )
    loads.append((pltpu.make_async_copy(own_hbm, own, sems.at[0, NB - 1]),))
    for load in loads[0] + loads[1]:
        load.start()
    sums = [None] * NB
    for a in range(NB - 1):
        for load in loads[a]:
            load.wait()
        if a + 2 < NB:
            for load in loads[a + 2]:
                load.start()
        lhs = jnp.concatenate(
            [received[:, OFF_AT[a, b]].reshape(size, lanes) for b in range(a + 1, NB)], axis=1
        )
        part = lax.dot_general(
            lhs, coeffs[a * size : (a + 1) * size], (((0,), (0,)), ((), ())), preferred_element_type=F32
        )
        for b in range(a + 1, NB):
            at = (b - a - 1) * lanes
            term = part[at : at + lanes]
            sums[b] = term if sums[b] is None else sums[b] + term
    loads[NB - 1][0].wait()
    for b in range(NB):
        both = own[b] if sums[b] is None else sums[b] + own[b]
        both = both.astype(BF16)
        out[b * half : (b + 1) * half, :occ] = both[:half]
        out[b * half : (b + 1) * half, occ:] = both[half:]


def strips_of(piece, cols):
    width = piece.shape[0] // NB
    full = lax.dot_general(piece[...], cols[...], (((1,), (1,)), ((), ())), preferred_element_type=F32).astype(BF16)
    for a in range(NB):
        begin = tile_of(a, a) * width
        yield begin, full[a * width : (a + 1) * width, a * width :]


def tiles_kernel(pieces, cols, out, place=0):
    high = out.shape[1]
    for piece in pieces:
        groups = piece.shape[0] // NB // high
        for begin, strip in strips_of(piece, cols):
            out[place : place + groups, :, begin : begin + strip.shape[1]] = strip.reshape(groups, high, strip.shape[1])
        place += groups


def near_kernel(own, sib, first, out):
    tiles_kernel((own, sib, first), own, out)


def cross_kernel(first, second, first_s, out_same, out_other):
    tiles_kernel((first,), second, out_same)
    tiles_kernel((first,), first_s, out_other)


def gather_kernel(near, own, first_s, second, second_s, far, far_s, out, late):
    cores = lax.axis_size("core")
    zs, ys = lax.axis_size("z"), lax.axis_size("y")
    x, core = lax.axis_index("x"), lax.axis_index("core")
    even = core == 0
    one, two = jnp.where(even, x ^ 1, x ^ 3), jnp.where(even, x ^ 3, x ^ 1)
    tiles_kernel((first_s, second, second_s), own, late)
    for chip, parity, source, begin in (
        (x, core, near, 0),
        (x, 1 - core, near, ys),
        (one, core, near, 2 * ys),
        (two, 1 - core, late, 0),
        (two, core, late, ys),
        (one, 1 - core, late, 2 * ys),
        (x ^ 2, core, far, 0),
        (x ^ 2, 1 - core, far_s, 0),
    ):
        z = chip * cores + parity
        for y in range(ys):
            out[jnp.where(even, z * ys + y, y * zs + z)] = source[begin + y]


def sum_of(received):
    total = received[0].astype(F32)
    for k in range(1, received.shape[0]):
        total = total + received[k].astype(F32)
    return total


def sum_kernel(received, out):
    out[...] = sum_of(received).astype(out.dtype)


def last_kernel(received, out):
    total = sum_of(received)
    width = out.shape[2]
    for t in range(out.shape[0]):
        out[t] = total[:, t * width : (t + 1) * width]


def body(integrals, orbitals):
    slabs, tile_count, width, size = integrals.shape
    occ = orbitals.shape[1]
    xs, cores, zs, ys = (lax.axis_size(name) for name in ("x", "core", "z", "y"))
    parts = xs * cores
    rows = size // (zs * ys)
    flops = 2 * slabs * width * size * occ

    packed = call(
        pack_kernel,
        jax.ShapeDtypeStruct((parts, len(OFF), width, slabs * width), BF16),
        (integrals,),
        0,
        2 * integrals.size * 2,
        63,
        in_specs=[ANY],
        out_specs=ANY,
        scratch_shapes=[
            pltpu.VMEM((slabs, len(OFF), width, size), BF16),
            pltpu.VMEM((parts, len(OFF), width, slabs * width), BF16),
            pltpu.SemaphoreType.DMA((2, NB - 1)),
        ],
    )
    received = lax.all_to_all(packed, ("x", "core"), 0, 0)
    own = call(
        own_kernel,
        jax.ShapeDtypeStruct((NB, slabs * width, occ), F32),
        (integrals, orbitals),
        flops * tile_count,
        2 * integrals.size + 2 * orbitals.size,
        63,
    )
    whole = jax.ShapeDtypeStruct((NB * width, slabs * occ), BF16)
    in_hbm = lambda array: pltpu.with_memory_space_constraint(array, pltpu.HBM)
    half = call(
        lower_kernel,
        whole,
        (in_hbm(received), in_hbm(orbitals), in_hbm(own)),
        flops * len(OFF),
        2 * received.size + 2 * orbitals.size,
        20,
        in_specs=[ANY] * 3,
        scratch_shapes=[
            pltpu.VMEM(received.shape, BF16),
            pltpu.VMEM(orbitals.shape, BF16),
            pltpu.VMEM(own.shape, F32),
            pltpu.SemaphoreType.DMA((2, NB)),
        ],
    )

    def exchange(array, turn, flip=0):
        pairs = [
            (x * cores + c, (x ^ (3 if (c + turn) % 2 else 1)) * cores + (c + flip) % cores)
            for x in range(xs)
            for c in range(cores)
        ]
        return lax.ppermute(array, ("x", "core"), pairs)

    def swapped(array):
        return lax.ppermute(array, "core", [(c, (c + 1) % cores) for c in range(cores)])

    product = 2 * half.shape[0] ** 2 * half.shape[1]
    tiles_shape = lambda pieces: jax.ShapeDtypeStruct((pieces * ys, rows, tile_count * width), BF16)
    first = exchange(half, 0)
    second = exchange(half, 1)
    sib = swapped(half)
    first_s = swapped(first)
    near = call(near_kernel, tiles_shape(3), (half, sib, first), 3 * product, 8 * half.size, 12)
    same, other = call(
        cross_kernel,
        (tiles_shape(1), tiles_shape(1)),
        (first, second, first_s),
        2 * product,
        7 * half.size,
        12,
    )
    far = exchange(same, 1)
    far_s = exchange(other, 1, 1)
    second_s = swapped(second)
    partial = call(
        gather_kernel,
        tiles_shape(zs),
        (near, half, first_s, second, second_s, far, far_s),
        3 * product,
        16 * half.size,
        16,
        scratch_shapes=[pltpu.VMEM(tiles_shape(3).shape, BF16)],
    )

    at = np.arange(zs * ys * parts).reshape(zs, ys, xs, cores)
    along_z = [[at[:, y, x, c].tolist() for x in range(xs) for y in range(ys)] for c in range(2)]
    along_y = [[at[z, :, x, c].tolist() for x in range(xs) for z in range(zs)] for c in range(2)]
    arrived = lax.all_to_all(
        partial.reshape(zs, ys * rows, tile_count * width), AXES, 0, 0, axis_index_groups=along_z[0] + along_y[1]
    )
    summed = call(
        sum_kernel,
        jax.ShapeDtypeStruct(arrived.shape[1:], BF16),
        (arrived,),
        arrived.size,
        2 * arrived.size,
        8,
    )
    arrived = lax.all_to_all(
        summed.reshape(ys, rows, tile_count * width), AXES, 0, 0, axis_index_groups=along_y[0] + along_z[1]
    )
    tiles = call(
        last_kernel,
        jax.ShapeDtypeStruct((tile_count, rows, width), F32),
        (arrived,),
        arrived.size,
        4 * arrived.size,
        8,
    )
    return jnp.transpose(tiles, (1, 0, 2))


def solution(mesh):
    grid = Mesh(mesh.devices.reshape(8, 8, 4, 2), AXES)
    return jax.shard_map(
        body,
        mesh=grid,
        in_specs=(P(("z", "y"), None, ("x", "core"), None), P()),
        out_specs=P(("z", "y"), None, ("x", "core")),
        check_vma=False,
    )
```

```python
import jax
import jax.numpy as jnp
import numpy as np
from jax import lax
from jax.experimental import pallas as pl
from jax.experimental.pallas import tpu as pltpu
from jax.sharding import Mesh
from jax.sharding import PartitionSpec as P


NB = 6
AXES = ("z", "y", "x", "core")
F32 = jnp.float32
BF16 = jnp.bfloat16
VMEM = pl.BlockSpec(memory_space=pltpu.VMEM)
ANY = pl.BlockSpec(memory_space=pl.ANY)


def tile_of(a, b):
    return a * NB - a * (a - 1) // 2 + b - a


OFF = [(a, b) for a in range(NB) for b in range(a + 1, NB)]
OFF_AT = {pair: at for at, pair in enumerate(OFF)}


def call(kernel, out_shape, args, flops, nbytes, vmem_mib, **options):
    options.setdefault("in_specs", [VMEM] * len(args))
    options.setdefault("out_specs", jax.tree.map(lambda _: VMEM, out_shape))
    return pl.pallas_call(
        kernel,
        out_shape=out_shape,
        compiler_params=pltpu.CompilerParams(vmem_limit_bytes=vmem_mib * 2**20),
        cost_estimate=pl.CostEstimate(flops=flops, bytes_accessed=nbytes, transcendentals=0),
        **options,
    )(*args)


def pack_kernel(tiles_hbm, out_hbm, tiles, out, sems):
    parts = out.shape[0]
    width = tiles.shape[3] // parts
    loads, stores = [], []
    for a in range(NB - 1):
        stored = pl.ds(tile_of(a, a + 1), NB - 1 - a)
        held = pl.ds(OFF_AT[a, a + 1], NB - 1 - a)
        loads.append(pltpu.make_async_copy(tiles_hbm.at[:, stored], tiles.at[:, held], sems.at[0, a]))
        stores.append(pltpu.make_async_copy(out.at[:, held], out_hbm.at[:, held], sems.at[1, a]))
    for load in loads:
        load.start()
    for at, (a, b) in enumerate(OFF):
        if b == a + 1:
            loads[a].wait()
        first, second = tiles[0, at], tiles[1, at]
        for d in range(parts):
            cols = slice(d * width, (d + 1) * width)
            out[d, at] = jnp.concatenate([first[:, cols], second[:, cols]], axis=1)
        if b == NB - 1:
            stores[a].start()
    for store in stores:
        store.wait()


def own_kernel(tiles, coeffs, out):
    size = tiles.shape[3]
    rows = 2 * tiles.shape[2]
    for m in range(NB):
        lhs = jnp.concatenate([tiles[:, tile_of(a, m)].reshape(rows, size) for a in range(m + 1)], axis=0)
        part = jnp.dot(lhs, coeffs[m * size : (m + 1) * size], preferred_element_type=F32)
        part = part.reshape(m + 1, rows, part.shape[1])
        if m:
            out[:m] = out[:m] + part[:m]
        out[m] = part[m]


def lower_kernel(received_hbm, coeffs_hbm, own_hbm, out, received, coeffs, own, sems):
    size = received.shape[0] * received.shape[2]
    lanes = received.shape[3]
    half = lanes // 2
    occ = coeffs.shape[1]
    loads = []
    for a in range(NB - 1):
        tiles = pl.ds(OFF_AT[a, a + 1], NB - 1 - a)
        rows = pl.ds(a * size, size)
        loads.append(
            (
                pltpu.make_async_copy(received_hbm.at[:, tiles], received.at[:, tiles], sems.at[0, a]),
                pltpu.make_async_copy(coeffs_hbm.at[rows], coeffs.at[rows], sems.at[1, a]),
            )
        )
    loads.append((pltpu.make_async_copy(own_hbm, own, sems.at[0, NB - 1]),))
    for load in loads[0] + loads[1]:
        load.start()
    sums = [None] * NB
    for a in range(NB - 1):
        for load in loads[a]:
            load.wait()
        if a + 2 < NB:
            for load in loads[a + 2]:
                load.start()
        lhs = jnp.concatenate(
            [received[:, OFF_AT[a, b]].reshape(size, lanes) for b in range(a + 1, NB)], axis=1
        )
        part = lax.dot_general(
            lhs, coeffs[a * size : (a + 1) * size], (((0,), (0,)), ((), ())), preferred_element_type=F32
        )
        for b in range(a + 1, NB):
            at = (b - a - 1) * lanes
            term = part[at : at + lanes]
            sums[b] = term if sums[b] is None else sums[b] + term
    loads[NB - 1][0].wait()
    for b in range(NB):
        both = own[b] if sums[b] is None else sums[b] + own[b]
        both = both.astype(BF16)
        out[b * half : (b + 1) * half, :occ] = both[:half]
        out[b * half : (b + 1) * half, occ:] = both[half:]


def strips_of(piece, cols):
    width = piece.shape[0] // NB
    full = lax.dot_general(piece[...], cols[...], (((1,), (1,)), ((), ())), preferred_element_type=F32).astype(BF16)
    for a in range(NB):
        begin = tile_of(a, a) * width
        yield begin, full[a * width : (a + 1) * width, a * width :]


def tiles_kernel(pieces, cols, out, place=0):
    high = out.shape[1]
    for piece in pieces:
        groups = piece.shape[0] // NB // high
        for begin, strip in strips_of(piece, cols):
            out[place : place + groups, :, begin : begin + strip.shape[1]] = strip.reshape(groups, high, strip.shape[1])
        place += groups


def near_kernel(own, sib, first, out):
    tiles_kernel((own, sib, first), own, out)


def cross_kernel(first, second, first_s, out_same, out_other):
    tiles_kernel((first,), second, out_same)
    tiles_kernel((first,), first_s, out_other)


def late_kernel(own, first_s, second, out):
    tiles_kernel((first_s, second), own, out)


def gather_kernel(near, late, own, second_s, far, far_s, out, last):
    cores = lax.axis_size("core")
    zs, ys = lax.axis_size("z"), lax.axis_size("y")
    x, core = lax.axis_index("x"), lax.axis_index("core")
    even = core == 0
    one, two = jnp.where(even, x ^ 1, x ^ 3), jnp.where(even, x ^ 3, x ^ 1)
    tiles_kernel((second_s,), own, last)
    for chip, parity, source, begin in (
        (x, core, near, 0),
        (x, 1 - core, near, ys),
        (one, core, near, 2 * ys),
        (two, 1 - core, late, 0),
        (two, core, late, ys),
        (one, 1 - core, last, 0),
        (x ^ 2, core, far, 0),
        (x ^ 2, 1 - core, far_s, 0),
    ):
        z = chip * cores + parity
        for y in range(ys):
            out[jnp.where(even, z * ys + y, y * zs + z)] = source[begin + y]


def sum_of(received):
    total = received[0].astype(F32)
    for k in range(1, received.shape[0]):
        total = total + received[k].astype(F32)
    return total


def sum_kernel(received, out):
    out[...] = sum_of(received).astype(out.dtype)


def last_kernel(received, out):
    total = sum_of(received)
    width = out.shape[2]
    for t in range(out.shape[0]):
        out[t] = total[:, t * width : (t + 1) * width]


def body(integrals, orbitals):
    slabs, tile_count, width, size = integrals.shape
    occ = orbitals.shape[1]
    xs, cores, zs, ys = (lax.axis_size(name) for name in ("x", "core", "z", "y"))
    parts = xs * cores
    rows = size // (zs * ys)
    flops = 2 * slabs * width * size * occ

    packed = call(
        pack_kernel,
        jax.ShapeDtypeStruct((parts, len(OFF), width, slabs * width), BF16),
        (integrals,),
        0,
        2 * integrals.size * 2,
        63,
        in_specs=[ANY],
        out_specs=ANY,
        scratch_shapes=[
            pltpu.VMEM((slabs, len(OFF), width, size), BF16),
            pltpu.VMEM((parts, len(OFF), width, slabs * width), BF16),
            pltpu.SemaphoreType.DMA((2, NB - 1)),
        ],
    )
    received = lax.all_to_all(packed, ("x", "core"), 0, 0)
    own = call(
        own_kernel,
        jax.ShapeDtypeStruct((NB, slabs * width, occ), F32),
        (integrals, orbitals),
        flops * tile_count,
        2 * integrals.size + 2 * orbitals.size,
        63,
    )
    whole = jax.ShapeDtypeStruct((NB * width, slabs * occ), BF16)
    in_hbm = lambda array: pltpu.with_memory_space_constraint(array, pltpu.HBM)
    half = call(
        lower_kernel,
        whole,
        (in_hbm(received), in_hbm(orbitals), in_hbm(own)),
        flops * len(OFF),
        2 * received.size + 2 * orbitals.size,
        20,
        in_specs=[ANY] * 3,
        scratch_shapes=[
            pltpu.VMEM(received.shape, BF16),
            pltpu.VMEM(orbitals.shape, BF16),
            pltpu.VMEM(own.shape, F32),
            pltpu.SemaphoreType.DMA((2, NB)),
        ],
    )

    def exchange(array, turn, flip=0):
        pairs = [
            (x * cores + c, (x ^ (3 if (c + turn) % 2 else 1)) * cores + (c + flip) % cores)
            for x in range(xs)
            for c in range(cores)
        ]
        return lax.ppermute(array, ("x", "core"), pairs)

    def swapped(array):
        return lax.ppermute(array, "core", [(c, (c + 1) % cores) for c in range(cores)])

    product = 2 * half.shape[0] ** 2 * half.shape[1]
    tiles_shape = lambda pieces: jax.ShapeDtypeStruct((pieces * ys, rows, tile_count * width), BF16)
    first = exchange(half, 0)
    second = exchange(half, 1)
    sib = swapped(half)
    first_s = swapped(first)
    near = call(near_kernel, tiles_shape(3), (half, sib, first), 3 * product, 8 * half.size, 12)
    same, other = call(
        cross_kernel,
        (tiles_shape(1), tiles_shape(1)),
        (first, second, first_s),
        2 * product,
        7 * half.size,
        12,
    )
    far = exchange(same, 1)
    far_s = exchange(other, 1, 1)
    second_s = swapped(second)
    late = call(late_kernel, tiles_shape(2), (half, first_s, second), 2 * product, 7 * half.size, 12)
    partial = call(
        gather_kernel,
        tiles_shape(zs),
        (near, late, half, second_s, far, far_s),
        product,
        16 * half.size,
        16,
        scratch_shapes=[pltpu.VMEM(tiles_shape(1).shape, BF16)],
    )

    at = np.arange(zs * ys * parts).reshape(zs, ys, xs, cores)
    along_z = [[at[:, y, x, c].tolist() for x in range(xs) for y in range(ys)] for c in range(2)]
    along_y = [[at[z, :, x, c].tolist() for x in range(xs) for z in range(zs)] for c in range(2)]
    arrived = lax.all_to_all(
        partial.reshape(zs, ys * rows, tile_count * width), AXES, 0, 0, axis_index_groups=along_z[0] + along_y[1]
    )
    summed = call(
        sum_kernel,
        jax.ShapeDtypeStruct(arrived.shape[1:], BF16),
        (arrived,),
        arrived.size,
        2 * arrived.size,
        8,
    )
    arrived = lax.all_to_all(
        summed.reshape(ys, rows, tile_count * width), AXES, 0, 0, axis_index_groups=along_y[0] + along_z[1]
    )
    tiles = call(
        last_kernel,
        jax.ShapeDtypeStruct((tile_count, rows, width), F32),
        (arrived,),
        arrived.size,
        4 * arrived.size,
        8,
    )
    return jnp.transpose(tiles, (1, 0, 2))


def solution(mesh):
    grid = Mesh(mesh.devices.reshape(8, 8, 4, 2), AXES)
    return jax.shard_map(
        body,
        mesh=grid,
        in_specs=(P(("z", "y"), None, ("x", "core"), None), P()),
        out_specs=P(("z", "y"), None, ("x", "core")),
        check_vma=False,
    )
```

```python
import jax
import jax.numpy as jnp
import numpy as np
from jax import lax
from jax.experimental import pallas as pl
from jax.experimental.pallas import tpu as pltpu
from jax.sharding import Mesh
from jax.sharding import PartitionSpec as P


NB = 6
AXES = ("z", "y", "x", "core")
F32 = jnp.float32
BF16 = jnp.bfloat16
VMEM = pl.BlockSpec(memory_space=pltpu.VMEM)
ANY = pl.BlockSpec(memory_space=pl.ANY)


def tile_of(a, b):
    return a * NB - a * (a - 1) // 2 + b - a


CUT = 4
OFF = [(a, b) for b in range(NB) for a in range(b)]
OFF_AT = {pair: at for at, pair in enumerate(OFF)}


def call(kernel, out_shape, args, flops, nbytes, vmem_mib, **options):
    options.setdefault("in_specs", [VMEM] * len(args))
    options.setdefault("out_specs", jax.tree.map(lambda _: VMEM, out_shape))
    return pl.pallas_call(
        kernel,
        out_shape=out_shape,
        compiler_params=pltpu.CompilerParams(vmem_limit_bytes=vmem_mib * 2**20),
        cost_estimate=pl.CostEstimate(flops=flops, bytes_accessed=nbytes, transcendentals=0),
        **options,
    )(*args)


def pack_kernel(tiles_hbm, out_hbm, tiles, out, sems):
    parts = out.shape[0]
    width = tiles.shape[3] // parts
    loads, stores = [], []
    for a in range(NB - 1):
        stored = pl.ds(tile_of(a, a + 1), NB - 1 - a)
        held = pl.ds(tile_of(a, a + 1) - a - 1, NB - 1 - a)
        loads.append(pltpu.make_async_copy(tiles_hbm.at[:, stored], tiles.at[:, held], sems.at[0, a]))
    for b in range(1, NB):
        ready = pl.ds(OFF_AT[0, b], b)
        stores.append(pltpu.make_async_copy(out.at[:, ready], out_hbm.at[:, ready], sems.at[1, b - 1]))
    for load in loads:
        load.start()
    for at, (a, b) in enumerate(OFF):
        if a == b - 1:
            loads[a].wait()
        first, second = (tiles[slab, tile_of(a, b) - a - 1] for slab in range(2))
        for d in range(parts):
            cols = slice(d * width, (d + 1) * width)
            out[d, at] = jnp.concatenate([first[:, cols], second[:, cols]], axis=1)
        if a == b - 1:
            stores[a].start()
    for store in stores:
        store.wait()


def own_kernel(tiles, coeffs, out):
    size = tiles.shape[3]
    rows = 2 * tiles.shape[2]
    for m in range(NB):
        lhs = jnp.concatenate([tiles[:, tile_of(a, m)].reshape(rows, size) for a in range(m + 1)], axis=0)
        part = jnp.dot(lhs, coeffs[m * size : (m + 1) * size], preferred_element_type=F32)
        part = part.reshape(m + 1, rows, part.shape[1])
        if m:
            out[:m] = out[:m] + part[:m]
        out[m] = part[m]


def lower_part(cols, received_hbm, coeffs_hbm, own_hbm, received, coeffs, own, sems):
    size = received.shape[0] * received.shape[2]
    lanes = received.shape[3]
    last = cols[-1]
    begin = OFF_AT[0, cols[0]] if cols[0] else 0
    count = OFF_AT[last - 1, last] + 1 - begin
    loads = [pltpu.make_async_copy(received_hbm.at[:, pl.ds(begin, count)], received, sems.at[0])]
    for a in range(last):
        rows = pl.ds(a * size, size)
        loads.append(pltpu.make_async_copy(coeffs_hbm.at[rows], coeffs.at[rows], sems.at[a + 1]))
    loads.append(pltpu.make_async_copy(own_hbm.at[pl.ds(cols[0], len(cols))], own, sems.at[last + 1]))
    for load in loads:
        load.start()
    loads[0].wait()
    sums = {b: None for b in cols}
    for a in range(last):
        loads[a + 1].wait()
        fed = [b for b in cols if b > a]
        lhs = jnp.concatenate(
            [received[:, OFF_AT[a, b] - begin].reshape(size, lanes) for b in fed], axis=1
        )
        part = lax.dot_general(
            lhs, coeffs[a * size : (a + 1) * size], (((0,), (0,)), ((), ())), preferred_element_type=F32
        )
        for at, b in enumerate(fed):
            term = part[at * lanes : (at + 1) * lanes]
            sums[b] = term if sums[b] is None else sums[b] + term
    loads[-1].wait()
    both = [own[at] if sums[b] is None else sums[b] + own[at] for at, b in enumerate(cols)]
    return [value.astype(BF16) for value in both]


def put_rows(values, out, begin):
    half, occ = values[0].shape[0] // 2, values[0].shape[1]
    for at, value in enumerate(values):
        rows = slice(begin + at * half, begin + (at + 1) * half)
        out[rows, :occ] = value[:half]
        out[rows, occ:] = value[half:]


def lower_a_kernel(received_hbm, coeffs_hbm, own_hbm, out_a, *scratch):
    put_rows(lower_part(range(CUT), received_hbm, coeffs_hbm, own_hbm, *scratch), out_a, 0)


def lower_b_kernel(received_hbm, coeffs_hbm, own_hbm, half_a, out, out_b, *scratch):
    values = lower_part(range(CUT, NB), received_hbm, coeffs_hbm, own_hbm, *scratch)
    put_rows(values, out_b, 0)
    out[: half_a.shape[0]] = half_a[...]
    put_rows(values, out, half_a.shape[0])


def rows_in(piece):
    return jnp.concatenate([part[...] for part in piece], axis=0) if isinstance(piece, tuple) else piece[...]


def strips_of(piece, cols):
    piece, cols = rows_in(piece), rows_in(cols)
    width = piece.shape[0] // NB
    full = lax.dot_general(piece, cols, (((1,), (1,)), ((), ())), preferred_element_type=F32).astype(BF16)
    for a in range(NB):
        begin = tile_of(a, a) * width
        yield begin, full[a * width : (a + 1) * width, a * width :]


def tiles_kernel(pieces, cols, out):
    place = 0
    high = out.shape[1]
    groups = out.shape[0] // len(pieces)
    for piece in pieces:
        for begin, strip in strips_of(piece, cols):
            out[place : place + groups, :, begin : begin + strip.shape[1]] = strip.reshape(groups, high, strip.shape[1])
        place += groups


def near_kernel(own, sib, first_a, first_b, out):
    tiles_kernel((own, sib, (first_a, first_b)), own, out)


def cross_kernel(first_a, first_b, second, first_as, first_bs, out_same, out_other):
    tiles_kernel(((first_a, first_b),), second, out_same)
    tiles_kernel(((first_a, first_b),), (first_as, first_bs), out_other)


def late_kernel(own, first_as, first_bs, second, out):
    tiles_kernel(((first_as, first_bs), second), own, out)


def gather_kernel(near, late, own, second_s, far, far_s, out, last):
    cores = lax.axis_size("core")
    zs, ys = lax.axis_size("z"), lax.axis_size("y")
    x, core = lax.axis_index("x"), lax.axis_index("core")
    even = core == 0
    one, two = jnp.where(even, x ^ 1, x ^ 3), jnp.where(even, x ^ 3, x ^ 1)
    tiles_kernel((second_s,), own, last)
    for chip, parity, source, begin in (
        (x, core, near, 0),
        (x, 1 - core, near, ys),
        (one, core, near, 2 * ys),
        (two, 1 - core, late, 0),
        (two, core, late, ys),
        (one, 1 - core, last, 0),
        (x ^ 2, core, far, 0),
        (x ^ 2, 1 - core, far_s, 0),
    ):
        z = chip * cores + parity
        for y in range(ys):
            out[jnp.where(even, z * ys + y, y * zs + z)] = source[begin + y]


def sum_of(received):
    total = received[0].astype(F32)
    for k in range(1, received.shape[0]):
        total = total + received[k].astype(F32)
    return total


def sum_kernel(received, out):
    out[...] = sum_of(received).astype(out.dtype)


def last_kernel(received, out):
    total = sum_of(received)
    width = out.shape[2]
    for t in range(out.shape[0]):
        out[t] = total[:, t * width : (t + 1) * width]


def body(integrals, orbitals):
    slabs, tile_count, width, size = integrals.shape
    occ = orbitals.shape[1]
    xs, cores, zs, ys = (lax.axis_size(name) for name in ("x", "core", "z", "y"))
    parts = xs * cores
    rows = size // (zs * ys)
    flops = 2 * slabs * width * size * occ

    packed = call(
        pack_kernel,
        jax.ShapeDtypeStruct((parts, len(OFF), width, slabs * width), BF16),
        (integrals,),
        0,
        2 * integrals.size * 2,
        63,
        in_specs=[ANY],
        out_specs=ANY,
        scratch_shapes=[
            pltpu.VMEM((slabs, len(OFF), width, size), BF16),
            pltpu.VMEM((parts, len(OFF), width, slabs * width), BF16),
            pltpu.SemaphoreType.DMA((2, NB - 1)),
        ],
    )
    received = lax.all_to_all(packed, ("x", "core"), 0, 0)
    own = call(
        own_kernel,
        jax.ShapeDtypeStruct((NB, slabs * width, occ), F32),
        (integrals, orbitals),
        flops * tile_count,
        2 * integrals.size + 2 * orbitals.size,
        63,
    )
    low = jax.ShapeDtypeStruct((CUT * width, slabs * occ), BF16)
    high = jax.ShapeDtypeStruct(((NB - CUT) * width, slabs * occ), BF16)
    whole = jax.ShapeDtypeStruct((NB * width, slabs * occ), BF16)
    in_hbm = [pltpu.with_memory_space_constraint(array, pltpu.HBM) for array in (received, orbitals, own)]

    def lower(kernel, out_shape, args, cols):
        tiles = sum(cols)
        return call(
            kernel,
            out_shape,
            (*in_hbm, *args),
            flops * tiles,
            2 * tiles * parts * width * slabs * width + 2 * orbitals.size,
            20,
            in_specs=[ANY] * 3 + [VMEM] * len(args),
            scratch_shapes=[
                pltpu.VMEM((parts, tiles, width, slabs * width), BF16),
                pltpu.VMEM((cols[-1] * size, occ), BF16),
                pltpu.VMEM((len(cols), slabs * width, occ), F32),
                pltpu.SemaphoreType.DMA((cols[-1] + 2,)),
            ],
        )

    def exchange(array, turn, flip=0):
        pairs = [
            (x * cores + c, (x ^ (3 if (c + turn) % 2 else 1)) * cores + (c + flip) % cores)
            for x in range(xs)
            for c in range(cores)
        ]
        return lax.ppermute(array, ("x", "core"), pairs)

    def swapped(array):
        return lax.ppermute(array, "core", [(c, (c + 1) % cores) for c in range(cores)])

    product = 2 * whole.shape[0] ** 2 * whole.shape[1]
    tiles_shape = lambda pieces: jax.ShapeDtypeStruct((pieces * ys, rows, tile_count * width), BF16)
    half_a = lower(lower_a_kernel, low, (), range(CUT))
    first_a = exchange(half_a, 0)
    half, half_b = lower(lower_b_kernel, (whole, high), (half_a,), range(CUT, NB))
    first_b = exchange(half_b, 0)
    second = exchange(half, 1)
    sib = swapped(half)
    first_as = swapped(first_a)
    first_bs = swapped(first_b)
    same, other = call(
        cross_kernel,
        (tiles_shape(1), tiles_shape(1)),
        (first_a, first_b, second, first_as, first_bs),
        2 * product,
        7 * half.size,
        12,
    )
    far = exchange(same, 1)
    far_s = exchange(other, 1, 1)
    second_s = swapped(second)
    near = call(near_kernel, tiles_shape(3), (half, sib, first_a, first_b), 3 * product, 8 * half.size, 12)
    late = call(
        late_kernel, tiles_shape(2), (half, first_as, first_bs, second), 2 * product, 7 * half.size, 12
    )
    partial = call(
        gather_kernel,
        tiles_shape(zs),
        (near, late, half, second_s, far, far_s),
        product,
        16 * half.size,
        16,
        scratch_shapes=[pltpu.VMEM(tiles_shape(1).shape, BF16)],
    )

    at = np.arange(zs * ys * parts).reshape(zs, ys, xs, cores)
    along_z = [[at[:, y, x, c].tolist() for x in range(xs) for y in range(ys)] for c in range(2)]
    along_y = [[at[z, :, x, c].tolist() for x in range(xs) for z in range(zs)] for c in range(2)]
    arrived = lax.all_to_all(
        partial.reshape(zs, ys * rows, tile_count * width), AXES, 0, 0, axis_index_groups=along_z[0] + along_y[1]
    )
    summed = call(
        sum_kernel,
        jax.ShapeDtypeStruct(arrived.shape[1:], BF16),
        (arrived,),
        arrived.size,
        2 * arrived.size,
        8,
    )
    arrived = lax.all_to_all(
        summed.reshape(ys, rows, tile_count * width), AXES, 0, 0, axis_index_groups=along_y[0] + along_z[1]
    )
    tiles = call(
        last_kernel,
        jax.ShapeDtypeStruct((tile_count, rows, width), F32),
        (arrived,),
        arrived.size,
        4 * arrived.size,
        8,
    )
    return jnp.transpose(tiles, (1, 0, 2))


def solution(mesh):
    grid = Mesh(mesh.devices.reshape(8, 8, 4, 2), AXES)
    return jax.shard_map(
        body,
        mesh=grid,
        in_specs=(P(("z", "y"), None, ("x", "core"), None), P()),
        out_specs=P(("z", "y"), None, ("x", "core")),
        check_vma=False,
    )
```

```python
import jax
import jax.numpy as jnp
import numpy as np
from jax import lax
from jax.experimental import pallas as pl
from jax.experimental.pallas import tpu as pltpu
from jax.sharding import Mesh
from jax.sharding import PartitionSpec as P


NB = 6
AXES = ("z", "y", "x", "core")
F32 = jnp.float32
BF16 = jnp.bfloat16
VMEM = pl.BlockSpec(memory_space=pltpu.VMEM)
ANY = pl.BlockSpec(memory_space=pl.ANY)


def tile_of(a, b):
    return a * NB - a * (a - 1) // 2 + b - a


CUT = 4
OFF = [(a, b) for b in range(NB) for a in range(b)]
OFF_AT = {pair: at for at, pair in enumerate(OFF)}


def call(kernel, out_shape, args, flops, nbytes, vmem_mib, **options):
    options.setdefault("in_specs", [VMEM] * len(args))
    options.setdefault("out_specs", jax.tree.map(lambda _: VMEM, out_shape))
    return pl.pallas_call(
        kernel,
        out_shape=out_shape,
        compiler_params=pltpu.CompilerParams(vmem_limit_bytes=vmem_mib * 2**20),
        cost_estimate=pl.CostEstimate(flops=flops, bytes_accessed=nbytes, transcendentals=0),
        **options,
    )(*args)


def pack_kernel(tiles_hbm, out_hbm, tiles, out, sems):
    parts = out.shape[0]
    width = tiles.shape[3] // parts
    loads, stores = [], []
    for a in range(NB - 1):
        stored = pl.ds(tile_of(a, a + 1), NB - 1 - a)
        held = pl.ds(tile_of(a, a + 1) - a - 1, NB - 1 - a)
        loads.append(pltpu.make_async_copy(tiles_hbm.at[:, stored], tiles.at[:, held], sems.at[0, a]))
    for b in range(1, NB):
        ready = pl.ds(OFF_AT[0, b], b)
        stores.append(pltpu.make_async_copy(out.at[:, ready], out_hbm.at[:, ready], sems.at[1, b - 1]))
    for load in loads:
        load.start()
    for at, (a, b) in enumerate(OFF):
        if a == b - 1:
            loads[a].wait()
        first, second = (tiles[slab, tile_of(a, b) - a - 1] for slab in range(2))
        for d in range(parts):
            cols = slice(d * width, (d + 1) * width)
            out[d, at] = jnp.concatenate([first[:, cols], second[:, cols]], axis=1)
        if a == b - 1:
            stores[a].start()
    for store in stores:
        store.wait()


def own_kernel(tiles, coeffs, out):
    size = tiles.shape[3]
    rows = 2 * tiles.shape[2]
    for m in range(NB):
        lhs = jnp.concatenate([tiles[:, tile_of(a, m)].reshape(rows, size) for a in range(m + 1)], axis=0)
        part = jnp.dot(lhs, coeffs[m * size : (m + 1) * size], preferred_element_type=F32)
        part = part.reshape(m + 1, rows, part.shape[1])
        if m:
            out[:m] = out[:m] + part[:m]
        out[m] = part[m]


def lower_part(cols, received_hbm, coeffs_hbm, own_hbm, received, coeffs, own, sems):
    size = received.shape[0] * received.shape[2]
    lanes = received.shape[3]
    last = cols[-1]
    begin = OFF_AT[0, cols[0]] if cols[0] else 0
    count = OFF_AT[last - 1, last] + 1 - begin
    loads = [pltpu.make_async_copy(received_hbm.at[:, pl.ds(begin, count)], received, sems.at[0])]
    for a in range(last):
        rows = pl.ds(a * size, size)
        loads.append(pltpu.make_async_copy(coeffs_hbm.at[rows], coeffs.at[rows], sems.at[a + 1]))
    loads.append(pltpu.make_async_copy(own_hbm.at[pl.ds(cols[0], len(cols))], own, sems.at[last + 1]))
    for load in loads:
        load.start()
    loads[0].wait()
    sums = {b: None for b in cols}
    for a in range(last):
        loads[a + 1].wait()
        fed = [b for b in cols if b > a]
        lhs = jnp.concatenate(
            [received[:, OFF_AT[a, b] - begin].reshape(size, lanes) for b in fed], axis=1
        )
        part = lax.dot_general(
            lhs, coeffs[a * size : (a + 1) * size], (((0,), (0,)), ((), ())), preferred_element_type=F32
        )
        for at, b in enumerate(fed):
            term = part[at * lanes : (at + 1) * lanes]
            sums[b] = term if sums[b] is None else sums[b] + term
    loads[-1].wait()
    both = [own[at] if sums[b] is None else sums[b] + own[at] for at, b in enumerate(cols)]
    return [value.astype(BF16) for value in both]


def put_rows(values, out, begin):
    half, occ = values[0].shape[0] // 2, values[0].shape[1]
    for at, value in enumerate(values):
        rows = slice(begin + at * half, begin + (at + 1) * half)
        out[rows, :occ] = value[:half]
        out[rows, occ:] = value[half:]


def lower_a_kernel(received_hbm, coeffs_hbm, own_hbm, out_a, *scratch):
    put_rows(lower_part(range(CUT), received_hbm, coeffs_hbm, own_hbm, *scratch), out_a, 0)


def lower_b_kernel(received_hbm, coeffs_hbm, own_hbm, half_a, out, out_b, *scratch):
    values = lower_part(range(CUT, NB), received_hbm, coeffs_hbm, own_hbm, *scratch)
    put_rows(values, out_b, 0)
    out[: half_a.shape[0]] = half_a[...]
    put_rows(values, out, half_a.shape[0])


def tiles_kernel(pieces, cols, out):
    width = cols.shape[0] // NB
    high = out.shape[1]
    groups = width // high
    right = cols[...]
    for place, piece in enumerate(pieces):
        for first, part in piece:
            full = lax.dot_general(
                part[...], right, (((1,), (1,)), ((), ())), preferred_element_type=F32
            ).astype(BF16)
            for k in range(part.shape[0] // width):
                a = first + k
                strip = full[k * width : (k + 1) * width, a * width :]
                begin = tile_of(a, a) * width
                out[place * groups : (place + 1) * groups, :, begin : begin + strip.shape[1]] = strip.reshape(
                    groups, high, strip.shape[1]
                )


def near_kernel(own, first_a, first_b, second, sib, out_mine, out_sib):
    pieces = ([(0, own)], [(0, first_a), (CUT, first_b)], [(0, second)])
    tiles_kernel(pieces, sib, out_sib)
    tiles_kernel(pieces, own, out_mine)


def far_kernel(far_a, far_b, cols, out):
    tiles_kernel(([(0, far_a), (CUT, far_b)],), cols, out)


def gather_kernel(near, far, near_s, far_s, out):
    cores = lax.axis_size("core")
    zs, ys = lax.axis_size("z"), lax.axis_size("y")
    x, core = lax.axis_index("x"), lax.axis_index("core")
    even = core == 0
    first, second = jnp.where(even, x ^ 1, x ^ 3), jnp.where(even, x ^ 3, x ^ 1)
    for places, source, parity in (
        ((x, first, second), near, core),
        ((x ^ 2,), far, core),
        ((x, second, first), near_s, 1 - core),
        ((x ^ 2,), far_s, 1 - core),
    ):
        for at, place in enumerate(places):
            z = place * cores + parity
            for y in range(ys):
                out[jnp.where(even, z * ys + y, y * zs + z)] = source[at * ys + y]


def sum_of(received):
    total = received[0].astype(F32)
    for k in range(1, received.shape[0]):
        total = total + received[k].astype(F32)
    return total


def sum_kernel(received, out):
    out[...] = sum_of(received).astype(out.dtype)


def last_kernel(received, out):
    total = sum_of(received)
    width = out.shape[2]
    for t in range(out.shape[0]):
        out[t] = total[:, t * width : (t + 1) * width]


def body(integrals, orbitals):
    slabs, tile_count, width, size = integrals.shape
    occ = orbitals.shape[1]
    xs, cores, zs, ys = (lax.axis_size(name) for name in ("x", "core", "z", "y"))
    parts = xs * cores
    rows = size // (zs * ys)
    flops = 2 * slabs * width * size * occ

    packed = call(
        pack_kernel,
        jax.ShapeDtypeStruct((parts, len(OFF), width, slabs * width), BF16),
        (integrals,),
        0,
        2 * integrals.size * 2,
        63,
        in_specs=[ANY],
        out_specs=ANY,
        scratch_shapes=[
            pltpu.VMEM((slabs, len(OFF), width, size), BF16),
            pltpu.VMEM((parts, len(OFF), width, slabs * width), BF16),
            pltpu.SemaphoreType.DMA((2, NB - 1)),
        ],
    )
    received = lax.all_to_all(packed, ("x", "core"), 0, 0)
    own = call(
        own_kernel,
        jax.ShapeDtypeStruct((NB, slabs * width, occ), F32),
        (integrals, orbitals),
        flops * tile_count,
        2 * integrals.size + 2 * orbitals.size,
        63,
    )
    low = jax.ShapeDtypeStruct((CUT * width, slabs * occ), BF16)
    high = jax.ShapeDtypeStruct(((NB - CUT) * width, slabs * occ), BF16)
    whole = jax.ShapeDtypeStruct((NB * width, slabs * occ), BF16)
    in_hbm = [pltpu.with_memory_space_constraint(array, pltpu.HBM) for array in (received, orbitals, own)]

    def lower(kernel, out_shape, args, cols):
        tiles = sum(cols)
        return call(
            kernel,
            out_shape,
            (*in_hbm, *args),
            flops * tiles,
            2 * tiles * parts * width * slabs * width + 2 * orbitals.size,
            20,
            in_specs=[ANY] * 3 + [VMEM] * len(args),
            scratch_shapes=[
                pltpu.VMEM((parts, tiles, width, slabs * width), BF16),
                pltpu.VMEM((cols[-1] * size, occ), BF16),
                pltpu.VMEM((len(cols), slabs * width, occ), F32),
                pltpu.SemaphoreType.DMA((cols[-1] + 2,)),
            ],
        )

    def exchange(array, turn):
        pairs = [((x, c), (x ^ (3 if (c + turn) % 2 else 1), c)) for x in range(xs) for c in range(cores)]
        return lax.ppermute(array, ("x", "core"), [(a * cores + c, b * cores + d) for (a, c), (b, d) in pairs])

    swap = [(i, (i + 1) % cores) for i in range(cores)]
    half_a = lower(lower_a_kernel, low, (), range(CUT))
    first_a = exchange(half_a, 0)
    half, half_b = lower(lower_b_kernel, (whole, high), (half_a,), range(CUT, NB))
    first_b = exchange(half_b, 0)
    second = exchange(half, 1)
    far_a = exchange(first_a, 1)
    sib = lax.ppermute(half, "core", swap)
    far_b = exchange(first_b, 1)

    product = 2 * half.shape[0] ** 2 * half.shape[1]
    near_shape = jax.ShapeDtypeStruct((3 * ys, rows, tile_count * width), BF16)
    far_shape = jax.ShapeDtypeStruct((ys, rows, tile_count * width), BF16)
    near, near_s = call(
        near_kernel,
        (near_shape, near_shape),
        (half, first_a, first_b, second, sib),
        6 * product,
        8 * half.size,
        16,
    )
    near_s = lax.ppermute(near_s, "core", swap)
    far_s = call(far_kernel, far_shape, (far_a, far_b, sib), product, 4 * half.size, 12)
    far_s = lax.ppermute(far_s, "core", swap)
    far = call(far_kernel, far_shape, (far_a, far_b, half), product, 4 * half.size, 12)
    partial = call(
        gather_kernel,
        jax.ShapeDtypeStruct((zs * ys, rows, tile_count * width), BF16),
        (near, far, near_s, far_s),
        0,
        8 * near.size,
        12,
    )

    at = np.arange(zs * ys * parts).reshape(zs, ys, xs, cores)
    along_z = [[at[:, y, x, c].tolist() for x in range(xs) for y in range(ys)] for c in range(2)]
    along_y = [[at[z, :, x, c].tolist() for x in range(xs) for z in range(zs)] for c in range(2)]
    arrived = lax.all_to_all(
        partial.reshape(zs, ys * rows, tile_count * width), AXES, 0, 0, axis_index_groups=along_z[0] + along_y[1]
    )
    summed = call(
        sum_kernel,
        jax.ShapeDtypeStruct(arrived.shape[1:], BF16),
        (arrived,),
        arrived.size,
        2 * arrived.size,
        8,
    )
    arrived = lax.all_to_all(
        summed.reshape(ys, rows, tile_count * width), AXES, 0, 0, axis_index_groups=along_y[0] + along_z[1]
    )
    tiles = call(
        last_kernel,
        jax.ShapeDtypeStruct((tile_count, rows, width), F32),
        (arrived,),
        arrived.size,
        4 * arrived.size,
        8,
    )
    return jnp.transpose(tiles, (1, 0, 2))


def solution(mesh):
    grid = Mesh(mesh.devices.reshape(8, 8, 4, 2), AXES)
    return jax.shard_map(
        body,
        mesh=grid,
        in_specs=(P(("z", "y"), None, ("x", "core"), None), P()),
        out_specs=P(("z", "y"), None, ("x", "core")),
        check_vma=False,
    )
```

```python
import jax
import jax.numpy as jnp
import numpy as np
from jax import lax
from jax.experimental import pallas as pl
from jax.experimental.pallas import tpu as pltpu
from jax.sharding import Mesh
from jax.sharding import PartitionSpec as P


NB = 6
AXES = ("z", "y", "x", "core")
F32 = jnp.float32
BF16 = jnp.bfloat16
VMEM = pl.BlockSpec(memory_space=pltpu.VMEM)
ANY = pl.BlockSpec(memory_space=pl.ANY)


def tile_of(a, b):
    return a * NB - a * (a - 1) // 2 + b - a


OFF = [(a, b) for a in range(NB) for b in range(a + 1, NB)]
OFF_AT = {pair: at for at, pair in enumerate(OFF)}


def call(kernel, out_shape, args, flops, nbytes, vmem_mib, **options):
    options.setdefault("in_specs", [VMEM] * len(args))
    options.setdefault("out_specs", jax.tree.map(lambda _: VMEM, out_shape))
    return pl.pallas_call(
        kernel,
        out_shape=out_shape,
        compiler_params=pltpu.CompilerParams(vmem_limit_bytes=vmem_mib * 2**20),
        cost_estimate=pl.CostEstimate(flops=flops, bytes_accessed=nbytes, transcendentals=0),
        **options,
    )(*args)


def pack_kernel(tiles_hbm, out_hbm, tiles, out, sems):
    parts = out.shape[0]
    width = tiles.shape[3] // parts
    loads, stores = [], []
    for a in range(NB - 1):
        stored = pl.ds(tile_of(a, a + 1), NB - 1 - a)
        held = pl.ds(OFF_AT[a, a + 1], NB - 1 - a)
        loads.append(pltpu.make_async_copy(tiles_hbm.at[:, stored], tiles.at[:, held], sems.at[0, a]))
        stores.append(pltpu.make_async_copy(out.at[:, held], out_hbm.at[:, held], sems.at[1, a]))
    for load in loads:
        load.start()
    for at, (a, b) in enumerate(OFF):
        if b == a + 1:
            loads[a].wait()
        first, second = tiles[0, at], tiles[1, at]
        for d in range(parts):
            cols = slice(d * width, (d + 1) * width)
            out[d, at] = jnp.concatenate([first[:, cols], second[:, cols]], axis=1)
        if b == NB - 1:
            stores[a].start()
    for store in stores:
        store.wait()


def own_kernel(tiles, coeffs, out):
    size = tiles.shape[3]
    rows = 2 * tiles.shape[2]
    for m in range(NB):
        lhs = jnp.concatenate([tiles[:, tile_of(a, m)].reshape(rows, size) for a in range(m + 1)], axis=0)
        part = jnp.dot(lhs, coeffs[m * size : (m + 1) * size], preferred_element_type=F32)
        part = part.reshape(m + 1, rows, part.shape[1])
        if m:
            out[:m] = out[:m] + part[:m]
        out[m] = part[m]


def lower_kernel(received_hbm, coeffs, own_hbm, out, out_a, out_b, received, own, sems):
    size = received.shape[0] * received.shape[2]
    lanes = received.shape[3]
    half = lanes // 2
    occ = coeffs.shape[1]
    loads = []
    for a in range(NB - 1):
        tiles = pl.ds(OFF_AT[a, a + 1], NB - 1 - a)
        loads.append(pltpu.make_async_copy(received_hbm.at[:, tiles], received.at[:, tiles], sems.at[a]))
    loads.append(pltpu.make_async_copy(own_hbm, own, sems.at[NB - 1]))
    for load in loads:
        load.start()
    sums = [None] * NB
    for a in range(NB - 1):
        loads[a].wait()
        lhs = jnp.concatenate(
            [received[:, OFF_AT[a, b]].reshape(size, lanes) for b in range(a + 1, NB)], axis=1
        )
        part = lax.dot_general(
            lhs, coeffs[a * size : (a + 1) * size], (((0,), (0,)), ((), ())), preferred_element_type=F32
        )
        for b in range(a + 1, NB):
            at = (b - a - 1) * lanes
            term = part[at : at + lanes]
            sums[b] = term if sums[b] is None else sums[b] + term
    loads[NB - 1].wait()
    for b in range(NB):
        both = own[b] if sums[b] is None else sums[b] + own[b]
        both = both.astype(BF16)
        for ref, at in ((out, b), (out_a if b < NB // 2 else out_b, b % (NB // 2))):
            ref[at * half : (at + 1) * half, :occ] = both[:half]
            ref[at * half : (at + 1) * half, occ:] = both[half:]


def products(pieces, cols, out):
    width = cols.shape[0] // NB
    high = out.shape[1]
    groups = width // high
    right = cols[...]
    for place, piece in enumerate(pieces):
        a = 0
        for part in piece:
            full = lax.dot_general(
                part[...], right, (((1,), (1,)), ((), ())), preferred_element_type=F32
            ).astype(BF16)
            for k in range(part.shape[0] // width):
                strip = full[k * width : (k + 1) * width, a * width :]
                begin = tile_of(a, a) * width
                out[place * groups : (place + 1) * groups, :, begin : begin + strip.shape[1]] = strip.reshape(
                    groups, high, strip.shape[1]
                )
                a += 1


def near_kernel(own, first_a, first_b, second, sib, out_mine, out_sib):
    pieces = ((own,), (first_a, first_b), (second,))
    products(pieces, sib, out_sib)
    products(pieces, own, out_mine)


def far_kernel(far_a, far_b, cols, out):
    products(((far_a, far_b),), cols, out)


def gather_kernel(near, far, near_s, far_s, out):
    cores = lax.axis_size("core")
    zs, ys = lax.axis_size("z"), lax.axis_size("y")
    x, core = lax.axis_index("x"), lax.axis_index("core")
    even = core == 0
    first, second = jnp.where(even, x ^ 1, x ^ 3), jnp.where(even, x ^ 3, x ^ 1)
    for places, source, parity in (
        ((x, first, second), near, core),
        ((x ^ 2,), far, core),
        ((x, second, first), near_s, 1 - core),
        ((x ^ 2,), far_s, 1 - core),
    ):
        for at, place in enumerate(places):
            z = place * cores + parity
            for y in range(ys):
                out[jnp.where(even, z * ys + y, y * zs + z)] = source[at * ys + y]


def sum_of(received):
    total = received[0].astype(F32)
    for k in range(1, received.shape[0]):
        total = total + received[k].astype(F32)
    return total


def sum_kernel(received, out):
    out[...] = sum_of(received).astype(out.dtype)


def last_kernel(received, out):
    total = sum_of(received)
    width = out.shape[2]
    for t in range(out.shape[0]):
        out[t] = total[:, t * width : (t + 1) * width]


def body(integrals, orbitals):
    slabs, tile_count, width, size = integrals.shape
    occ = orbitals.shape[1]
    xs, cores, zs, ys = (lax.axis_size(name) for name in ("x", "core", "z", "y"))
    parts = xs * cores
    rows = size // (zs * ys)
    flops = 2 * slabs * width * size * occ

    packed = call(
        pack_kernel,
        jax.ShapeDtypeStruct((parts, len(OFF), width, slabs * width), BF16),
        (integrals,),
        0,
        2 * integrals.size * 2,
        63,
        in_specs=[ANY],
        out_specs=ANY,
        scratch_shapes=[
            pltpu.VMEM((slabs, len(OFF), width, size), BF16),
            pltpu.VMEM((parts, len(OFF), width, slabs * width), BF16),
            pltpu.SemaphoreType.DMA((2, NB - 1)),
        ],
    )
    received = lax.all_to_all(packed, ("x", "core"), 0, 0)
    own = call(
        own_kernel,
        jax.ShapeDtypeStruct((NB, slabs * width, occ), F32),
        (integrals, orbitals),
        flops * tile_count,
        2 * integrals.size + 2 * orbitals.size,
        52,
    )
    whole = jax.ShapeDtypeStruct((NB * width, slabs * occ), BF16)
    side = jax.ShapeDtypeStruct((NB // 2 * width, slabs * occ), BF16)
    in_hbm = lambda array: pltpu.with_memory_space_constraint(array, pltpu.HBM)
    half, half_a, half_b = call(
        lower_kernel,
        (whole, side, side),
        (in_hbm(received), orbitals, in_hbm(own)),
        flops * len(OFF),
        2 * received.size + 2 * orbitals.size,
        16,
        in_specs=[ANY, VMEM, ANY],
        scratch_shapes=[
            pltpu.VMEM(received.shape, BF16),
            pltpu.VMEM(own.shape, F32),
            pltpu.SemaphoreType.DMA((NB,)),
        ],
    )

    def exchange(array, turn):
        pairs = [((x, c), (x ^ (3 if (c + turn) % 2 else 1), c)) for x in range(xs) for c in range(cores)]
        return lax.ppermute(array, ("x", "core"), [(a * cores + c, b * cores + d) for (a, c), (b, d) in pairs])

    swap = [(i, (i + 1) % cores) for i in range(cores)]
    first_a = exchange(half_a, 0)
    first_b = exchange(half_b, 0)
    second = exchange(half, 1)
    far_a = exchange(first_a, 1)
    sib = lax.ppermute(half, "core", swap)
    far_b = exchange(first_b, 1)

    product = 2 * half.shape[0] ** 2 * half.shape[1]
    near_shape = jax.ShapeDtypeStruct((3 * ys, rows, tile_count * width), BF16)
    far_shape = jax.ShapeDtypeStruct((ys, rows, tile_count * width), BF16)
    near, near_s = call(
        near_kernel,
        (near_shape, near_shape),
        (half, first_a, first_b, second, sib),
        6 * product,
        8 * half.size,
        16,
    )
    near_s = lax.ppermute(near_s, "core", swap)
    far_s = call(far_kernel, far_shape, (far_a, far_b, sib), product, 4 * half.size, 12)
    far_s = lax.ppermute(far_s, "core", swap)
    far = call(far_kernel, far_shape, (far_a, far_b, half), product, 4 * half.size, 12)
    partial = call(
        gather_kernel,
        jax.ShapeDtypeStruct((zs * ys, rows, tile_count * width), BF16),
        (near, far, near_s, far_s),
        0,
        8 * near.size,
        12,
    )

    at = np.arange(zs * ys * parts).reshape(zs, ys, xs, cores)
    along_z = [[at[:, y, x, c].tolist() for x in range(xs) for y in range(ys)] for c in range(2)]
    along_y = [[at[z, :, x, c].tolist() for x in range(xs) for z in range(zs)] for c in range(2)]
    arrived = lax.all_to_all(
        partial.reshape(zs, ys * rows, tile_count * width), AXES, 0, 0, axis_index_groups=along_z[0] + along_y[1]
    )
    summed = call(
        sum_kernel,
        jax.ShapeDtypeStruct(arrived.shape[1:], BF16),
        (arrived,),
        arrived.size,
        2 * arrived.size,
        8,
    )
    arrived = lax.all_to_all(
        summed.reshape(ys, rows, tile_count * width), AXES, 0, 0, axis_index_groups=along_y[0] + along_z[1]
    )
    tiles = call(
        last_kernel,
        jax.ShapeDtypeStruct((tile_count, rows, width), F32),
        (arrived,),
        arrived.size,
        4 * arrived.size,
        8,
    )
    return jnp.transpose(tiles, (1, 0, 2))


def solution(mesh):
    grid = Mesh(mesh.devices.reshape(8, 8, 4, 2), AXES)
    return jax.shard_map(
        body,
        mesh=grid,
        in_specs=(P(("z", "y"), None, ("x", "core"), None), P()),
        out_specs=P(("z", "y"), None, ("x", "core")),
        check_vma=False,
    )
```

```python
import jax
import jax.numpy as jnp
import numpy as np
from jax import lax
from jax.experimental import pallas as pl
from jax.experimental.pallas import tpu as pltpu
from jax.sharding import Mesh
from jax.sharding import PartitionSpec as P


NB = 6
AXES = ("z", "y", "x", "core")
F32 = jnp.float32
BF16 = jnp.bfloat16
VMEM = pl.BlockSpec(memory_space=pltpu.VMEM)
ANY = pl.BlockSpec(memory_space=pl.ANY)


def tile_of(a, b):
    return a * NB - a * (a - 1) // 2 + b - a


OFF = [(a, b) for a in range(NB) for b in range(a + 1, NB)]
OFF_AT = {pair: at for at, pair in enumerate(OFF)}


def call(kernel, out_shape, args, flops, nbytes, vmem_mib, **options):
    options.setdefault("in_specs", [VMEM] * len(args))
    options.setdefault("out_specs", jax.tree.map(lambda _: VMEM, out_shape))
    return pl.pallas_call(
        kernel,
        out_shape=out_shape,
        compiler_params=pltpu.CompilerParams(vmem_limit_bytes=vmem_mib * 2**20),
        cost_estimate=pl.CostEstimate(flops=flops, bytes_accessed=nbytes, transcendentals=0),
        **options,
    )(*args)


def pack_kernel(tiles_hbm, out_hbm, tiles, out, sems):
    parts = out.shape[0]
    width = tiles.shape[3] // parts
    loads, stores = [], []
    for a in range(NB - 1):
        stored = pl.ds(tile_of(a, a + 1), NB - 1 - a)
        held = pl.ds(OFF_AT[a, a + 1], NB - 1 - a)
        loads.append(pltpu.make_async_copy(tiles_hbm.at[:, stored], tiles.at[:, held], sems.at[0, a]))
        stores.append(pltpu.make_async_copy(out.at[:, held], out_hbm.at[:, held], sems.at[1, a]))
    for load in loads:
        load.start()
    for at, (a, b) in enumerate(OFF):
        if b == a + 1:
            loads[a].wait()
        first, second = tiles[0, at], tiles[1, at]
        for d in range(parts):
            cols = slice(d * width, (d + 1) * width)
            out[d, at] = jnp.concatenate([first[:, cols], second[:, cols]], axis=1)
        if b == NB - 1:
            stores[a].start()
    for store in stores:
        store.wait()


def own_kernel(tiles, coeffs, out):
    size = tiles.shape[3]
    rows = 2 * tiles.shape[2]
    for m in range(NB):
        lhs = jnp.concatenate([tiles[:, tile_of(a, m)].reshape(rows, size) for a in range(m + 1)], axis=0)
        part = jnp.dot(lhs, coeffs[m * size : (m + 1) * size], preferred_element_type=F32)
        part = part.reshape(m + 1, rows, part.shape[1])
        if m:
            out[:m] = out[:m] + part[:m]
        out[m] = part[m]


def lower_kernel(received_hbm, coeffs, own, out, out_a, out_b, received, sems):
    size = received.shape[0] * received.shape[2]
    lanes = received.shape[3]
    half = lanes // 2
    occ = coeffs.shape[1]
    loads = []
    for a in range(NB - 1):
        tiles = pl.ds(OFF_AT[a, a + 1], NB - 1 - a)
        loads.append(pltpu.make_async_copy(received_hbm.at[:, tiles], received.at[:, tiles], sems.at[a]))
    for load in loads:
        load.start()
    sums = [None] * NB
    for a in range(NB - 1):
        loads[a].wait()
        lhs = jnp.concatenate(
            [received[:, OFF_AT[a, b]].reshape(size, lanes) for b in range(a + 1, NB)], axis=1
        )
        part = lax.dot_general(
            lhs, coeffs[a * size : (a + 1) * size], (((0,), (0,)), ((), ())), preferred_element_type=F32
        )
        for b in range(a + 1, NB):
            at = (b - a - 1) * lanes
            term = part[at : at + lanes]
            sums[b] = term if sums[b] is None else sums[b] + term
    for b in range(NB):
        both = own[b] if sums[b] is None else sums[b] + own[b]
        both = both.astype(BF16)
        for ref, at in ((out, b), (out_a if b < NB // 2 else out_b, b % (NB // 2))):
            ref[at * half : (at + 1) * half, :occ] = both[:half]
            ref[at * half : (at + 1) * half, occ:] = both[half:]


def products(pieces, cols, out):
    width = cols.shape[0] // NB
    high = out.shape[1]
    groups = width // high
    right = cols[...]
    for place, piece in enumerate(pieces):
        a = 0
        for part in piece:
            full = lax.dot_general(
                part[...], right, (((1,), (1,)), ((), ())), preferred_element_type=F32
            ).astype(BF16)
            for k in range(part.shape[0] // width):
                strip = full[k * width : (k + 1) * width, a * width :]
                begin = tile_of(a, a) * width
                out[place * groups : (place + 1) * groups, :, begin : begin + strip.shape[1]] = strip.reshape(
                    groups, high, strip.shape[1]
                )
                a += 1


def near_kernel(own, first_a, first_b, second, sib, out_mine, out_sib):
    pieces = ((own,), (first_a, first_b), (second,))
    products(pieces, sib, out_sib)
    products(pieces, own, out_mine)


def far_kernel(far_a, far_b, cols, out):
    products(((far_a, far_b),), cols, out)


def gather_kernel(near, far, near_s, far_s, out):
    cores = lax.axis_size("core")
    zs, ys = lax.axis_size("z"), lax.axis_size("y")
    x, core = lax.axis_index("x"), lax.axis_index("core")
    even = core == 0
    first, second = jnp.where(even, x ^ 1, x ^ 3), jnp.where(even, x ^ 3, x ^ 1)
    for places, source, parity in (
        ((x, first, second), near, core),
        ((x ^ 2,), far, core),
        ((x, second, first), near_s, 1 - core),
        ((x ^ 2,), far_s, 1 - core),
    ):
        for at, place in enumerate(places):
            z = place * cores + parity
            for y in range(ys):
                out[jnp.where(even, z * ys + y, y * zs + z)] = source[at * ys + y]


def sum_of(received):
    total = received[0].astype(F32)
    for k in range(1, received.shape[0]):
        total = total + received[k].astype(F32)
    return total


def sum_kernel(received, out):
    out[...] = sum_of(received).astype(out.dtype)


def last_kernel(received, out):
    total = sum_of(received)
    width = out.shape[2]
    for t in range(out.shape[0]):
        out[t] = total[:, t * width : (t + 1) * width]


def body(integrals, orbitals):
    slabs, tile_count, width, size = integrals.shape
    occ = orbitals.shape[1]
    xs, cores, zs, ys = (lax.axis_size(name) for name in ("x", "core", "z", "y"))
    parts = xs * cores
    rows = size // (zs * ys)
    flops = 2 * slabs * width * size * occ

    packed = call(
        pack_kernel,
        jax.ShapeDtypeStruct((parts, len(OFF), width, slabs * width), BF16),
        (integrals,),
        0,
        2 * integrals.size * 2,
        63,
        in_specs=[ANY],
        out_specs=ANY,
        scratch_shapes=[
            pltpu.VMEM((slabs, len(OFF), width, size), BF16),
            pltpu.VMEM((parts, len(OFF), width, slabs * width), BF16),
            pltpu.SemaphoreType.DMA((2, NB - 1)),
        ],
    )
    received = lax.all_to_all(packed, ("x", "core"), 0, 0)
    own = call(
        own_kernel,
        jax.ShapeDtypeStruct((NB, slabs * width, occ), F32),
        (integrals, orbitals),
        flops * tile_count,
        2 * integrals.size + 2 * orbitals.size,
        52,
    )
    whole = jax.ShapeDtypeStruct((NB * width, slabs * occ), BF16)
    side = jax.ShapeDtypeStruct((NB // 2 * width, slabs * occ), BF16)
    in_hbm = lambda array: pltpu.with_memory_space_constraint(array, pltpu.HBM)
    half, half_a, half_b = call(
        lower_kernel,
        (whole, side, side),
        (in_hbm(received), orbitals, own),
        flops * len(OFF),
        2 * received.size + 2 * orbitals.size,
        16,
        in_specs=[ANY, VMEM, VMEM],
        scratch_shapes=[
            pltpu.VMEM(received.shape, BF16),
            pltpu.SemaphoreType.DMA((NB - 1,)),
        ],
    )

    def exchange(array, turn):
        pairs = [((x, c), (x ^ (3 if (c + turn) % 2 else 1), c)) for x in range(xs) for c in range(cores)]
        return lax.ppermute(array, ("x", "core"), [(a * cores + c, b * cores + d) for (a, c), (b, d) in pairs])

    swap = [(i, (i + 1) % cores) for i in range(cores)]
    first_a = exchange(half_a, 0)
    first_b = exchange(half_b, 0)
    second = exchange(half, 1)
    far_a = exchange(first_a, 1)
    sib = lax.ppermute(half, "core", swap)
    far_b = exchange(first_b, 1)

    product = 2 * half.shape[0] ** 2 * half.shape[1]
    near_shape = jax.ShapeDtypeStruct((3 * ys, rows, tile_count * width), BF16)
    far_shape = jax.ShapeDtypeStruct((ys, rows, tile_count * width), BF16)
    near, near_s = call(
        near_kernel,
        (near_shape, near_shape),
        (half, first_a, first_b, second, sib),
        6 * product,
        8 * half.size,
        16,
    )
    near_s = lax.ppermute(near_s, "core", swap)
    far_s = call(far_kernel, far_shape, (far_a, far_b, sib), product, 4 * half.size, 12)
    far_s = lax.ppermute(far_s, "core", swap)
    far = call(far_kernel, far_shape, (far_a, far_b, half), product, 4 * half.size, 12)
    partial = call(
        gather_kernel,
        jax.ShapeDtypeStruct((zs * ys, rows, tile_count * width), BF16),
        (near, far, near_s, far_s),
        0,
        8 * near.size,
        12,
    )

    at = np.arange(zs * ys * parts).reshape(zs, ys, xs, cores)
    along_z = [[at[:, y, x, c].tolist() for x in range(xs) for y in range(ys)] for c in range(2)]
    along_y = [[at[z, :, x, c].tolist() for x in range(xs) for z in range(zs)] for c in range(2)]
    arrived = lax.all_to_all(
        partial.reshape(zs, ys * rows, tile_count * width), AXES, 0, 0, axis_index_groups=along_z[0] + along_y[1]
    )
    summed = call(
        sum_kernel,
        jax.ShapeDtypeStruct(arrived.shape[1:], BF16),
        (arrived,),
        arrived.size,
        2 * arrived.size,
        8,
    )
    arrived = lax.all_to_all(
        summed.reshape(ys, rows, tile_count * width), AXES, 0, 0, axis_index_groups=along_y[0] + along_z[1]
    )
    tiles = call(
        last_kernel,
        jax.ShapeDtypeStruct((tile_count, rows, width), F32),
        (arrived,),
        arrived.size,
        4 * arrived.size,
        8,
    )
    return jnp.transpose(tiles, (1, 0, 2))


def solution(mesh):
    grid = Mesh(mesh.devices.reshape(8, 8, 4, 2), AXES)
    return jax.shard_map(
        body,
        mesh=grid,
        in_specs=(P(("z", "y"), None, ("x", "core"), None), P()),
        out_specs=P(("z", "y"), None, ("x", "core")),
        check_vma=False,
    )
```

```python
import jax
import jax.numpy as jnp
import numpy as np
from jax import lax
from jax.experimental import pallas as pl
from jax.experimental.pallas import tpu as pltpu
from jax.sharding import Mesh
from jax.sharding import PartitionSpec as P


NB = 6
CUT = 4
AXES = ("z", "y", "x", "core")
F32 = jnp.float32
BF16 = jnp.bfloat16
VMEM = pl.BlockSpec(memory_space=pltpu.VMEM)
ANY = pl.BlockSpec(memory_space=pl.ANY)


def tile_of(a, b):
    return a * NB - a * (a - 1) // 2 + b - a


OFF = [(a, b) for a in range(NB) for b in range(a + 1, NB)]
OFF_AT = {pair: at for at, pair in enumerate(OFF)}


def call(kernel, out_shape, args, flops, nbytes, vmem_mib, **options):
    options.setdefault("in_specs", [VMEM] * len(args))
    options.setdefault("out_specs", jax.tree.map(lambda _: VMEM, out_shape))
    return pl.pallas_call(
        kernel,
        out_shape=out_shape,
        compiler_params=pltpu.CompilerParams(vmem_limit_bytes=vmem_mib * 2**20),
        cost_estimate=pl.CostEstimate(flops=flops, bytes_accessed=nbytes, transcendentals=0),
        **options,
    )(*args)


def pack_kernel(tiles_hbm, out_hbm, tiles, out, sems):
    parts = out.shape[0]
    width = tiles.shape[3] // parts
    loads, stores = [], []
    for a in range(NB - 1):
        stored = pl.ds(tile_of(a, a + 1), NB - 1 - a)
        held = pl.ds(OFF_AT[a, a + 1], NB - 1 - a)
        loads.append(pltpu.make_async_copy(tiles_hbm.at[:, stored], tiles.at[:, held], sems.at[0, a]))
        stores.append(pltpu.make_async_copy(out.at[:, held], out_hbm.at[:, held], sems.at[1, a]))
    for load in loads:
        load.start()
    for at, (a, b) in enumerate(OFF):
        if b == a + 1:
            loads[a].wait()
        first, second = tiles[0, at], tiles[1, at]
        for d in range(parts):
            cols = slice(d * width, (d + 1) * width)
            out[d, at] = jnp.concatenate([first[:, cols], second[:, cols]], axis=1)
        if b == NB - 1:
            stores[a].start()
    for store in stores:
        store.wait()


def own_kernel(tiles, coeffs, out):
    size = tiles.shape[3]
    rows = 2 * tiles.shape[2]
    for m in range(NB):
        lhs = jnp.concatenate([tiles[:, tile_of(a, m)].reshape(rows, size) for a in range(m + 1)], axis=0)
        part = jnp.dot(lhs, coeffs[m * size : (m + 1) * size], preferred_element_type=F32)
        part = part.reshape(m + 1, rows, part.shape[1])
        if m:
            out[:m] = out[:m] + part[:m]
        out[m] = part[m]


def lower_kernel(received_hbm, coeffs, own, out, out_a, out_b, received, sems):
    size = received.shape[0] * received.shape[2]
    lanes = received.shape[3]
    half = lanes // 2
    occ = coeffs.shape[1]
    loads = []
    for a in range(NB - 1):
        tiles = pl.ds(OFF_AT[a, a + 1], NB - 1 - a)
        loads.append(pltpu.make_async_copy(received_hbm.at[:, tiles], received.at[:, tiles], sems.at[a]))
    for load in loads:
        load.start()
    sums = [None] * NB
    for a in range(NB - 1):
        loads[a].wait()
        lhs = jnp.concatenate(
            [received[:, OFF_AT[a, b]].reshape(size, lanes) for b in range(a + 1, NB)], axis=1
        )
        part = lax.dot_general(
            lhs, coeffs[a * size : (a + 1) * size], (((0,), (0,)), ((), ())), preferred_element_type=F32
        )
        for b in range(a + 1, NB):
            at = (b - a - 1) * lanes
            term = part[at : at + lanes]
            sums[b] = term if sums[b] is None else sums[b] + term
    for b in range(NB):
        both = own[b] if sums[b] is None else sums[b] + own[b]
        both = both.astype(BF16)
        for ref, at in ((out, b), (out_a, b) if b < CUT else (out_b, b - CUT)):
            ref[at * half : (at + 1) * half, :occ] = both[:half]
            ref[at * half : (at + 1) * half, occ:] = both[half:]


def products(pieces, cols, out):
    width = cols.shape[0] // NB
    high = out.shape[1]
    groups = width // high
    right = cols[...]
    for place, piece in enumerate(pieces):
        a = 0
        for part in piece:
            full = lax.dot_general(
                part[...], right, (((1,), (1,)), ((), ())), preferred_element_type=F32
            ).astype(BF16)
            for k in range(part.shape[0] // width):
                strip = full[k * width : (k + 1) * width, a * width :]
                begin = tile_of(a, a) * width
                out[place * groups : (place + 1) * groups, :, begin : begin + strip.shape[1]] = strip.reshape(
                    groups, high, strip.shape[1]
                )
                a += 1


def near_kernel(own, first_a, first_b, second, sib, out_mine, out_sib):
    pieces = ((own,), (first_a, first_b), (second,))
    products(pieces, sib, out_sib)
    products(pieces, own, out_mine)


def far_kernel(far_a, far_b, cols, out):
    products(((far_a, far_b),), cols, out)


def gather_kernel(near, far, near_s, far_s, out):
    cores = lax.axis_size("core")
    zs, ys = lax.axis_size("z"), lax.axis_size("y")
    x, core = lax.axis_index("x"), lax.axis_index("core")
    even = core == 0
    first, second = jnp.where(even, x ^ 1, x ^ 3), jnp.where(even, x ^ 3, x ^ 1)
    for places, source, parity in (
        ((x, first, second), near, core),
        ((x ^ 2,), far, core),
        ((x, second, first), near_s, 1 - core),
        ((x ^ 2,), far_s, 1 - core),
    ):
        for at, place in enumerate(places):
            z = place * cores + parity
            for y in range(ys):
                out[jnp.where(even, z * ys + y, y * zs + z)] = source[at * ys + y]


def sum_of(received):
    total = received[0].astype(F32)
    for k in range(1, received.shape[0]):
        total = total + received[k].astype(F32)
    return total


def sum_kernel(received, out):
    out[...] = sum_of(received).astype(out.dtype)


def last_kernel(received, out):
    total = sum_of(received)
    width = out.shape[2]
    for t in range(out.shape[0]):
        out[t] = total[:, t * width : (t + 1) * width]


def body(integrals, orbitals):
    slabs, tile_count, width, size = integrals.shape
    occ = orbitals.shape[1]
    xs, cores, zs, ys = (lax.axis_size(name) for name in ("x", "core", "z", "y"))
    parts = xs * cores
    rows = size // (zs * ys)
    flops = 2 * slabs * width * size * occ

    packed = call(
        pack_kernel,
        jax.ShapeDtypeStruct((parts, len(OFF), width, slabs * width), BF16),
        (integrals,),
        0,
        2 * integrals.size * 2,
        63,
        in_specs=[ANY],
        out_specs=ANY,
        scratch_shapes=[
            pltpu.VMEM((slabs, len(OFF), width, size), BF16),
            pltpu.VMEM((parts, len(OFF), width, slabs * width), BF16),
            pltpu.SemaphoreType.DMA((2, NB - 1)),
        ],
    )
    received = lax.all_to_all(packed, ("x", "core"), 0, 0)
    own = call(
        own_kernel,
        jax.ShapeDtypeStruct((NB, slabs * width, occ), F32),
        (integrals, orbitals),
        flops * tile_count,
        2 * integrals.size + 2 * orbitals.size,
        52,
    )
    whole = jax.ShapeDtypeStruct((NB * width, slabs * occ), BF16)
    low = jax.ShapeDtypeStruct((CUT * width, slabs * occ), BF16)
    high = jax.ShapeDtypeStruct(((NB - CUT) * width, slabs * occ), BF16)
    in_hbm = lambda array: pltpu.with_memory_space_constraint(array, pltpu.HBM)
    half, half_a, half_b = call(
        lower_kernel,
        (whole, low, high),
        (in_hbm(received), orbitals, own),
        flops * len(OFF),
        2 * received.size + 2 * orbitals.size,
        16,
        in_specs=[ANY, VMEM, VMEM],
        scratch_shapes=[
            pltpu.VMEM(received.shape, BF16),
            pltpu.SemaphoreType.DMA((NB - 1,)),
        ],
    )

    def exchange(array, turn):
        pairs = [((x, c), (x ^ (3 if (c + turn) % 2 else 1), c)) for x in range(xs) for c in range(cores)]
        return lax.ppermute(array, ("x", "core"), [(a * cores + c, b * cores + d) for (a, c), (b, d) in pairs])

    swap = [(i, (i + 1) % cores) for i in range(cores)]
    first_a = exchange(half_a, 0)
    first_b = exchange(half_b, 0)
    second = exchange(half, 1)
    far_a = exchange(first_a, 1)
    sib = lax.ppermute(half, "core", swap)
    far_b = exchange(first_b, 1)

    product = 2 * half.shape[0] ** 2 * half.shape[1]
    near_shape = jax.ShapeDtypeStruct((3 * ys, rows, tile_count * width), BF16)
    far_shape = jax.ShapeDtypeStruct((ys, rows, tile_count * width), BF16)
    near, near_s = call(
        near_kernel,
        (near_shape, near_shape),
        (half, first_a, first_b, second, sib),
        6 * product,
        8 * half.size,
        16,
    )
    near_s = lax.ppermute(near_s, "core", swap)
    far_s = call(far_kernel, far_shape, (far_a, far_b, sib), product, 4 * half.size, 12)
    far_s = lax.ppermute(far_s, "core", swap)
    far = call(far_kernel, far_shape, (far_a, far_b, half), product, 4 * half.size, 12)
    partial = call(
        gather_kernel,
        jax.ShapeDtypeStruct((zs * ys, rows, tile_count * width), BF16),
        (near, far, near_s, far_s),
        0,
        8 * near.size,
        12,
    )

    at = np.arange(zs * ys * parts).reshape(zs, ys, xs, cores)
    along_z = [[at[:, y, x, c].tolist() for x in range(xs) for y in range(ys)] for c in range(2)]
    along_y = [[at[z, :, x, c].tolist() for x in range(xs) for z in range(zs)] for c in range(2)]
    arrived = lax.all_to_all(
        partial.reshape(zs, ys * rows, tile_count * width), AXES, 0, 0, axis_index_groups=along_z[0] + along_y[1]
    )
    summed = call(
        sum_kernel,
        jax.ShapeDtypeStruct(arrived.shape[1:], BF16),
        (arrived,),
        arrived.size,
        2 * arrived.size,
        8,
    )
    arrived = lax.all_to_all(
        summed.reshape(ys, rows, tile_count * width), AXES, 0, 0, axis_index_groups=along_y[0] + along_z[1]
    )
    tiles = call(
        last_kernel,
        jax.ShapeDtypeStruct((tile_count, rows, width), F32),
        (arrived,),
        arrived.size,
        4 * arrived.size,
        8,
    )
    return jnp.transpose(tiles, (1, 0, 2))


def solution(mesh):
    grid = Mesh(mesh.devices.reshape(8, 8, 4, 2), AXES)
    return jax.shard_map(
        body,
        mesh=grid,
        in_specs=(P(("z", "y"), None, ("x", "core"), None), P()),
        out_specs=P(("z", "y"), None, ("x", "core")),
        check_vma=False,
    )
```
